128 devices in a mesh: leaf: 4 (over y), rows: 32 (over z, x, core).
Axes of the slice: x: 4, y: 4, z: 4, core: 2. Of those that a mesh axis runs over, the one named last changes fastest.
Arguments:
- leaf_rhs: float32 [8, 16, 2048], P(None, 'leaf', 'rows'), may hold values from -6 to 6
- parent_rhs: float32 [8, 4, 4096], P(None, 'leaf', 'rows'), may hold values from -6 to 6
- root_rhs: float32 [8, 4096], P(None, ('leaf', 'rows')), may hold values from -6 to 6
- leaf_inv: bfloat16 [16, 2048, 2048], P('leaf', 'rows'), as said below
- leaf_panel: bfloat16 [16, 8192, 2048], P('leaf', 'rows'), may hold values from -0.0625 to 0.0625
- leaf_rows: int32 [16, 8192], P('leaf', 'rows'), may hold values from 0 to 8191, as said below
- leaf_height: int32 [16], P('leaf'), may hold values from 2048 to 8192
- parent_inv: bfloat16 [4, 4096, 4096], P('leaf', 'rows'), as said below
- parent_panel: bfloat16 [4, 4096, 4096], P('leaf', 'rows'), may hold values from -0.046875 to 0.046875
- parent_rows: int32 [4, 4096], P('leaf', 'rows'), may hold values from 0 to 4095, as said below
- parent_height: int32 [4], P('leaf'), may hold values from 1024 to 4096
- root_inv: bfloat16 [4096, 4096], P('rows'), as said below
Outputs:
- leaf_solution: float32 [8, 16, 2048], P(None, 'leaf', 'rows')
- parent_solution: float32 [8, 4, 4096], P(None, 'leaf', 'rows')
- root_solution: float32 [8, 4096], P(None, ('leaf', 'rows'))
The draws below stay inside these ranges and needn't reach their ends.
Inputs may be any that keep to these rules, and one draw needn't show every extreme that they name: `leaf_rows`: each leaf's first leaf_height entries are distinct and ascending; every entry is a valid ancestor index. `parent_rows`: each parent's first parent_height entries are distinct and ascending. `leaf_inv`: A dense well conditioned matrix. `parent_inv`: A dense well conditioned matrix. `root_inv`: A dense well conditioned matrix.
All inputs are finite; a program needn't handle non-finite values.
Results may differ from the reference program's by a relative error of at most 0.009.
Values may be sent and summed in bfloat16 or wider, within the bound.
A program may use at most 64 MiB of HBM per device.

```python
import jax
import jax.numpy as jnp
from jax import lax

R = 8
WL = 2048
WP = 4096
WR = 4096
PARENTS = 4
LEAVES = 16
HL = 8192
HP = 4096


def subset_rows(key, count, length):
    k_one, k_two, k_three = jax.random.split(key, 3)
    heights = jax.random.randint(k_one, (count,), length // 4, length + 1)
    order = jax.random.permutation(k_two, count)
    heights = heights.at[order[0]].set(length).at[order[1]].set(length // 4)
    perms = jax.vmap(lambda kk: jax.random.permutation(kk, length))(jax.random.split(k_three, count))
    ranks = jnp.argsort(perms, axis=1)
    places = jnp.arange(length)[None, :]
    chosen = ranks < heights[:, None]
    keyvals = jnp.where(chosen, places, places + length)
    rows_out = jnp.argsort(keyvals, axis=1).astype(jnp.int32)
    return (rows_out, heights.astype(jnp.int32))


def leaf_struct(key):
    return subset_rows(jax.random.fold_in(key, 11), LEAVES, HL)


def parent_struct(key):
    return subset_rows(jax.random.fold_in(key, 23), PARENTS, HP)


def inverse_draw(key, count, width):
    noise = jax.random.normal(key, (count, width, width), jnp.float32)
    eye = jnp.eye(width, dtype=jnp.float32)[None, :, :]
    return (eye + 0.3 * noise / jnp.sqrt(width * 1.0)).astype(jnp.bfloat16)


def draw_leaf_rows(key, part):
    return leaf_struct(key)[0]


def draw_leaf_height(key, part):
    return leaf_struct(key)[1]


def draw_parent_rows(key, part):
    return parent_struct(key)[0]


def draw_parent_height(key, part):
    return parent_struct(key)[1]


def draw_leaf_inv(key, part):
    return inverse_draw(jax.random.fold_in(key, 31), LEAVES, WL)


def draw_parent_inv(key, part):
    return inverse_draw(jax.random.fold_in(key, 37), PARENTS, WP)


def draw_root_inv(key, part):
    return inverse_draw(jax.random.fold_in(key, 41), 1, WR)[0]


def level_of(key, dims, cuts, low, high):
    level = 1.0
    for axis_at, shards_of in cuts:
        steps = jax.random.uniform(jax.random.fold_in(jax.random.fold_in(key, 6), axis_at), (shards_of,), jnp.float32, low / len(cuts), high / len(cuts))
        level = level * jnp.repeat(jnp.exp(steps), dims[axis_at] // shards_of).reshape((-1,) + (1,) * (len(dims) - 1 - axis_at))
    return level


def scatter_about(rng, dims, scale, limit, cuts=(), kind=jnp.bfloat16):
    loudness = level_of(rng, dims, cuts, -0.22, 0.18) if cuts else 1.0
    drawn = jax.random.normal(rng, dims, jnp.float32) * scale * loudness
    return jnp.minimum(jnp.maximum(drawn, -limit), limit).astype(kind)


def setup_inputs(seed: int = 0) -> dict:
    key_list = jax.random.split(jax.random.key(seed), 13)
    return {
        "leaf_rhs": scatter_about(key_list[0], (R, LEAVES, WL), 1.0, 6.0, ((1, 4), (2, 32)), jnp.float32),
        "parent_rhs": scatter_about(key_list[1], (R, PARENTS, WP), 1.0, 6.0, ((1, 4), (2, 32)), jnp.float32),
        "root_rhs": scatter_about(key_list[2], (R, WR), 1.0, 6.0, ((1, 128),), jnp.float32),
        "leaf_inv": draw_leaf_inv(jax.random.fold_in(key_list[12], 71), 0),
        "leaf_panel": scatter_about(key_list[4], (LEAVES, HL, WL), (4 * WL) ** -0.5, 0.0625, ((0, 4), (1, 32))),
        "leaf_rows": draw_leaf_rows(jax.random.fold_in(key_list[12], 71), 0),
        "leaf_height": draw_leaf_height(jax.random.fold_in(key_list[12], 71), 0),
        "parent_inv": draw_parent_inv(jax.random.fold_in(key_list[12], 71), 0),
        "parent_panel": scatter_about(key_list[8], (PARENTS, HP, WP), (4 * WP) ** -0.5, 0.046875, ((0, 4), (1, 32))),
        "parent_rows": draw_parent_rows(jax.random.fold_in(key_list[12], 71), 0),
        "parent_height": draw_parent_height(jax.random.fold_in(key_list[12], 71), 0),
        "root_inv": draw_root_inv(jax.random.fold_in(key_list[12], 71), 0),
    }


def fdot(left, right):
    return jnp.dot(left.astype(jnp.float32), right.astype(jnp.float32), preferred_element_type=jnp.float32)


def reference(leaf_rhs, parent_rhs, root_rhs, leaf_inv, leaf_panel, leaf_rows, leaf_height, parent_inv, parent_panel, parent_rows, parent_height, root_inv):
    lb = jnp.moveaxis(leaf_rhs.astype(jnp.bfloat16), 1, 0)

    def apply_inv(args):
        vec, inverse = args
        return fdot(vec, inverse.T)

    ly = lax.map(apply_inv, (lb, leaf_inv))
    lyb = ly.astype(jnp.bfloat16)
    leaf_pos = jnp.arange(HL)

    def leaf_up(args):
        vec, panel, rows, height = args
        update = fdot(vec, panel.T)
        update = jnp.where(leaf_pos[None, :] < height, update, 0.0)
        return jnp.zeros((R, HL), jnp.float32).at[:, rows].add(update)

    acc = lax.map(leaf_up, (lyb, leaf_panel, leaf_rows, leaf_height))
    pacc = acc[:, :, :WP].reshape(PARENTS, 4, R, WP).sum(1)
    racc = acc[:, :, WP:].sum(0)
    prb = (jnp.moveaxis(parent_rhs, 1, 0) - pacc).astype(jnp.bfloat16)
    py = lax.map(apply_inv, (prb, parent_inv))
    pyb = py.astype(jnp.bfloat16)
    parent_pos = jnp.arange(HP)

    def parent_up(args):
        vec, panel, rows, height = args
        update = fdot(vec, panel.T)
        update = jnp.where(parent_pos[None, :] < height, update, 0.0)
        return jnp.zeros((R, WR), jnp.float32).at[:, rows].add(update)

    racc_two = lax.map(parent_up, (pyb, parent_panel, parent_rows, parent_height)).sum(0)
    rrb = (root_rhs - racc - racc_two).astype(jnp.bfloat16)
    ry = fdot(rrb, root_inv.T)
    root_solution = fdot(ry.astype(jnp.bfloat16), root_inv)
    rxb = root_solution.astype(jnp.bfloat16)

    def parent_back(args):
        partial_value, panel, rows, height, inverse = args
        ancestor = rxb[:, rows]
        ancestor = jnp.where(parent_pos[None, :] < height, ancestor, jnp.zeros_like(ancestor))
        term = fdot(ancestor, panel)
        value = (partial_value - term).astype(jnp.bfloat16)
        return fdot(value, inverse)

    px = lax.map(parent_back, (py, parent_panel, parent_rows, parent_height, parent_inv))
    pxb = jnp.repeat(px.astype(jnp.bfloat16), 4, axis=0)

    def leaf_back(args):
        partial_value, upper, panel, rows, height, inverse = args
        whole = jnp.concatenate([upper, rxb], axis=1)
        ancestor = whole[:, rows]
        ancestor = jnp.where(leaf_pos[None, :] < height, ancestor, jnp.zeros_like(ancestor))
        term = fdot(ancestor, panel)
        value = (partial_value - term).astype(jnp.bfloat16)
        return fdot(value, inverse)

    lx = lax.map(leaf_back, (ly, pxb, leaf_panel, leaf_rows, leaf_height, leaf_inv))
    return jnp.moveaxis(lx, 0, 1), jnp.moveaxis(px, 0, 1), root_solution
```

```python
import functools

import jax
import jax.numpy as jnp
from jax import lax
from jax.experimental import pallas as pl
from jax.experimental.pallas import tpu as pltpu
from jax.sharding import PartitionSpec as P

F32 = jnp.float32
BF16 = jnp.bfloat16
LANES = 128
HALF = 64
NT = (((1,), (1,)), ((), ()))
PHASES = 15


def dot(a, b):
    return jnp.dot(a, b, preferred_element_type=F32)


def dot_nt(a, b):
    return lax.dot_general(a, b, NT, preferred_element_type=F32)


def swap_halves(x):
    return pltpu.roll(x, HALF, 1)


def kernel(
    n,
    groups,
    leaf_rhs,
    parent_rhs,
    root_rhs,
    leaf_rows,
    leaf_height,
    parent_rows,
    parent_height,
    leaf_inv_hbm,
    leaf_panel_hbm,
    parent_inv_hbm,
    parent_panel_hbm,
    root_inv_hbm,
    leaf_out,
    parent_out,
    root_out,
    leaf_inv,
    leaf_panel,
    parent_inv,
    parent_panel,
    root_inv,
    onehot,
    onehot_p,
    xs,
    spread_hi,
    spread_lo,
    terms,
    g1,
    g2,
    s3,
    r3,
    g4,
    g5,
    s6,
    r6,
    g7a,
    g7b,
    s8,
    r8,
    g9,
    s10,
    r10,
    s11,
    r11,
    g12,
    s13,
    r13,
    s14,
    r14,
    load_sem,
    send_sem,
    recv_sem,
):
    group = lax.axis_index("leaf")
    me = lax.axis_index("rows")

    barrier = pltpu.get_barrier_semaphore()

    def greet_row(i, carry):
        pl.semaphore_signal(barrier, inc=1, device_id={"rows": lax.rem(me + i, n)})
        return carry

    lax.fori_loop(1, n, greet_row, 0)
    for i in range(1, groups):
        pl.semaphore_signal(barrier, inc=1, device_id={"leaf": lax.rem(group + i, groups)})

    loads = [
        pltpu.make_async_copy(src, dst, load_sem.at[i])
        for i, (src, dst) in enumerate(
            (
                (leaf_inv_hbm, leaf_inv),
                (leaf_panel_hbm, leaf_panel),
                (parent_inv_hbm, parent_inv),
                (parent_panel_hbm, parent_panel),
                (root_inv_hbm, root_inv),
            )
        )
    ]
    for copy in loads:
        copy.start()

    low = lax.broadcasted_iota(jnp.int32, (8, LANES), 1) < HALF
    low16 = lax.broadcasted_iota(jnp.int32, (16, LANES), 1) < HALF

    def drain(ref, sem, count):
        view = ref.at[pl.ds(0, count)]
        pltpu.make_async_copy(view, view, sem).wait()

    def gather_start(ref, value, phase):
        ref[me] = value

        def send(i, carry):
            pltpu.make_async_remote_copy(
                src_ref=ref.at[me],
                dst_ref=ref.at[me],
                send_sem=send_sem.at[phase],
                recv_sem=recv_sem.at[phase],
                device_id={"rows": lax.rem(me + i, n)},
            ).start()
            return carry

        lax.fori_loop(1, n, send, 0)

    def gather_wait(ref, phase):
        drain(ref, recv_sem.at[phase], n - 1)

    def scatter_start(src, dst, phase):
        def send(i, carry):
            peer = lax.rem(me + i, n)
            pltpu.make_async_remote_copy(
                src_ref=src.at[peer],
                dst_ref=dst.at[me],
                send_sem=send_sem.at[phase],
                recv_sem=recv_sem.at[phase],
                device_id={"rows": peer},
            ).start()
            return carry

        lax.fori_loop(1, n, send, 0)
        dst[me] = src[me]

    def scatter_sum(dst, phase):
        drain(dst, recv_sem.at[phase], n - 1)
        return jnp.sum(dst[...], axis=0)

    def pack_rhs():
        tops = [
            jnp.concatenate([leaf_rhs[:, 2 * a, :], leaf_rhs[:, 2 * a + 1, :]], axis=1)
            for a in range(2)
        ]
        return jnp.concatenate(tops, axis=0).astype(BF16)

    def unpack(ref):
        for c in range(n // 2):
            even = ref[2 * c].astype(F32)
            odd = ref[2 * c + 1].astype(F32)
            cols = pl.ds(c * LANES, LANES)
            xs[0:16, cols] = jnp.where(low16, even, swap_halves(odd)).astype(BF16)
            xs[16:32, cols] = jnp.where(low16, swap_halves(even), odd).astype(BF16)

    def pack_terms(dst):
        for c in range(n // 2):
            cols = pl.ds(c * LANES, LANES)
            for a in range(2):
                rows = pl.ds(8 * a, 8)
                even = terms[pl.ds(16 * a, 8), cols]
                odd = terms[pl.ds(16 * a + 8, 8), cols]
                dst[2 * c, rows, :] = jnp.where(low, even, swap_halves(odd))
                dst[2 * c + 1, rows, :] = jnp.where(low, swap_halves(even), odd)

    def columns(ref):
        return jnp.concatenate([ref[c] for c in range(n)], axis=1)

    def spread(value, where_at, blocks, width):
        high = value.astype(BF16).astype(F32)
        rest = value - high
        for q in range(0, blocks, 2):
            rows = pl.ds(8 * q, 16)
            for part, ref in ((high, spread_hi), (rest, spread_lo)):
                pair = [jnp.where(where_at == q + k, part, 0.0) for k in range(2)]
                ref[rows, 0:width] = jnp.concatenate(pair, axis=0).astype(BF16)

    def pick(table, where_at, first):
        total = jnp.zeros(where_at.shape, F32)
        for q in range(n):
            total += jnp.where(where_at == first + q, table[8 * q : 8 * q + 8, :], 0.0)
        return total

    packed_rhs = pack_rhs()
    pl.semaphore_wait(barrier, n - 1 + groups - 1)
    gather_start(g1, packed_rhs, 0)

    piece = leaf_rows.shape[1]
    at_list, low_list = [], []
    for s in range(4):
        rows_s = leaf_rows[s : s + 1, :]
        pos = me * piece + lax.broadcasted_iota(jnp.int32, (1, piece), 1)
        at_list.append(jnp.where(pos < leaf_height[s], rows_s >> 7, -1))
        low_list.append(rows_s & (LANES - 1))
    height = 4 * piece
    leaf_at = jnp.broadcast_to(jnp.concatenate(at_list, axis=1), (8, height))
    leaf_low = jnp.concatenate(low_list, axis=1)
    onehot[...] = jnp.where(
        lax.broadcasted_iota(jnp.int32, (LANES, height), 0) == leaf_low, 1.0, 0.0
    ).astype(BF16)
    rows_p = parent_rows[...]
    pos_p = me * LANES + lax.broadcasted_iota(jnp.int32, (1, LANES), 1)
    parent_at = jnp.broadcast_to(
        jnp.where(pos_p < parent_height[0], rows_p >> 7, -1), (8, LANES)
    )
    onehot_p[...] = jnp.where(
        lax.broadcasted_iota(jnp.int32, (LANES, LANES), 0) == (rows_p & (LANES - 1)), 1.0, 0.0
    ).astype(BF16)

    loads[0].wait()
    gather_wait(g1, 0)
    unpack(g1)
    full = dot_nt(xs[...], leaf_inv[...])
    ly = jnp.concatenate(
        [
            jnp.where(low, full[0:8, 0:LANES], full[16:24, 0:LANES]),
            jnp.where(low, full[8:16, LANES:], full[24:32, LANES:]),
        ],
        axis=0,
    )
    gather_start(g2, ly.astype(BF16), 1)
    loads[1].wait()
    gather_wait(g2, 1)
    unpack(g2)
    updates = []
    for s in range(4):
        a, b = s // 2, s % 2
        got = dot_nt(xs[16 * b : 16 * b + 16, :], leaf_panel[pl.ds(s * piece, piece), :])
        updates.append(got[8 * a : 8 * a + 8, :])
    spread(jnp.concatenate(updates, axis=1), leaf_at, 2 * n, height)
    acc = dot_nt(spread_hi[...], onehot[...]) + dot_nt(spread_lo[...], onehot[...])
    for q in range(2 * n):
        s3[q % n, q // n] = acc[8 * q : 8 * q + 8, :]
    width = root_rhs.shape[1]
    per_slab = LANES // width
    slab = lax.div(group * n + me, per_slab)
    part = lax.rem(me, per_slab)
    lane_part = lax.broadcasted_iota(jnp.int32, (8, LANES), 1) // width
    mine = jnp.concatenate([root_rhs[...]] * per_slab, axis=1)
    s3[slab, 1] = s3[slab, 1] - jnp.where(lane_part == part, mine, 0.0)
    scatter_start(s3, r3, 2)
    sums = scatter_sum(r3, 2)

    prb = (parent_rhs[...] - sums[0]).astype(BF16)
    gather_start(g4, prb, 3)
    loads[2].wait()
    gather_wait(g4, 3)
    py = dot_nt(columns(g4), parent_inv[...])
    gather_start(g5, py.astype(BF16), 4)
    loads[3].wait()
    gather_wait(g5, 4)
    pupd = dot_nt(columns(g5), parent_panel[...])
    spread(pupd, parent_at, n, LANES)
    acc_p = dot_nt(spread_hi[0 : 8 * n, 0:LANES], onehot_p[...]) + dot_nt(
        spread_lo[0 : 8 * n, 0:LANES], onehot_p[...]
    )
    for q in range(n):
        s6[q] = acc_p[8 * q : 8 * q + 8, :]
    scatter_start(s6, r6, 5)
    partial = scatter_sum(r6, 5) + sums[1]

    g7a[group] = partial
    for i in range(1, groups):
        pltpu.make_async_remote_copy(
            src_ref=g7a.at[group],
            dst_ref=g7a.at[group],
            send_sem=send_sem.at[6],
            recv_sem=recv_sem.at[6],
            device_id={"leaf": lax.rem(group + i, groups)},
        ).start()
    drain(g7a, recv_sem.at[6], groups - 1)
    rrb = (-jnp.sum(g7a[...], axis=0)).astype(BF16)
    gather_start(g7b, rrb, 7)
    loads[4].wait()
    gather_wait(g7b, 7)
    ry = dot_nt(columns(g7b), root_inv[...])
    root_term = dot(ry.astype(BF16), root_inv[...])
    for c in range(n):
        s8[c] = root_term[:, c * LANES : (c + 1) * LANES]
    scatter_start(s8, r8, 8)
    root_slab = scatter_sum(r8, 8)
    gather_start(g9, root_slab.astype(BF16), 9)
    gather_wait(g9, 9)

    rxb = g9[...].reshape(n * 8, LANES)
    parent_anc = pick(dot(rxb, onehot_p[...]), parent_at, 0).astype(BF16)
    parent_term = dot(parent_anc, parent_panel[...])
    for c in range(n):
        s10[c] = parent_term[:, c * LANES : (c + 1) * LANES]
    scatter_start(s10, r10, 10)
    leaf_anc = pick(dot(rxb, onehot[...]), leaf_at, n)
    mine = jnp.where(lane_part == part, g9[slab].astype(F32), 0.0)
    root_out[...] = functools.reduce(
        lambda x, y: x + y, [mine[:, k * width : (k + 1) * width] for k in range(per_slab)]
    )
    pvb = (py - scatter_sum(r10, 10)).astype(BF16)
    parent_term = dot(pvb, parent_inv[...])
    for c in range(n):
        s11[c] = parent_term[:, c * LANES : (c + 1) * LANES]
    scatter_start(s11, r11, 11)
    parent_sol = scatter_sum(r11, 11)
    parent_out[...] = parent_sol
    gather_start(g12, parent_sol.astype(BF16), 12)
    gather_wait(g12, 12)

    pxb = g12[...].reshape(n * 8, LANES)
    leaf_anc = (leaf_anc + pick(dot(pxb, onehot[...]), leaf_at, 0)).astype(BF16)
    for s in range(4):
        terms[pl.ds(8 * s, 8), :] = dot(
            leaf_anc[:, s * piece : (s + 1) * piece], leaf_panel[pl.ds(s * piece, piece), :]
        )
    pack_terms(s13)
    scatter_start(s13, r13, 13)
    lvb = ly - scatter_sum(r13, 13)
    none = jnp.zeros((8, LANES), F32)
    blocks = []
    for s in range(4):
        a, b = s // 2, s % 2
        held = jnp.where(low if b == 0 else ~low, lvb[8 * a : 8 * a + 8, :], 0.0)
        blocks.append(jnp.concatenate([held, none] if a == 0 else [none, held], axis=1))
    terms[...] = dot(jnp.concatenate(blocks, axis=0).astype(BF16), leaf_inv[...])
    pack_terms(s14)
    scatter_start(s14, r14, 14)
    leaf_out[...] = scatter_sum(r14, 14)

    for phase, ref in enumerate(
        (g1, g2, r3, g4, g5, r6, g7a, g7b, r8, g9, r10, r11, g12, r13, r14)
    ):
        drain(ref, send_sem.at[phase], (groups if phase == 6 else n) - 1)


def solution(mesh):
    n = mesh.shape["rows"]
    groups = mesh.shape["leaf"]

    def shards(
        leaf_rhs,
        parent_rhs,
        root_rhs,
        leaf_inv,
        leaf_panel,
        leaf_rows,
        leaf_height,
        parent_inv,
        parent_panel,
        parent_rows,
        parent_height,
        root_inv,
    ):
        leaf_cols = leaf_inv.shape[2]
        cols = root_inv.shape[1]
        height = 4 * leaf_panel.shape[1]
        packed = (16, LANES)
        vmem = pl.BlockSpec(memory_space=pltpu.VMEM)
        smem = pl.BlockSpec(memory_space=pltpu.SMEM)
        hbm = pl.BlockSpec(memory_space=pl.ANY)
        slabs = (n, 8, LANES)
        buffers = [
            ((n, *packed), BF16),
            ((n, *packed), BF16),
            ((n, 2, 8, LANES), F32),
            ((n, 2, 8, LANES), F32),
            (slabs, BF16),
            (slabs, BF16),
            (slabs, F32),
            (slabs, F32),
            ((groups, 8, LANES), F32),
            (slabs, BF16),
            (slabs, F32),
            (slabs, F32),
            (slabs, BF16),
            (slabs, F32),
            (slabs, F32),
            (slabs, F32),
            (slabs, F32),
            (slabs, BF16),
            ((n, *packed), F32),
            ((n, *packed), F32),
            ((n, *packed), F32),
            ((n, *packed), F32),
        ]
        leaf_out, parent_out, root_out = pl.pallas_call(
            functools.partial(kernel, n, groups),
            out_shape=(
                jax.ShapeDtypeStruct(packed, F32),
                jax.ShapeDtypeStruct((8, LANES), F32),
                jax.ShapeDtypeStruct(root_rhs.shape, F32),
            ),
            in_specs=[vmem, vmem, vmem, vmem, smem, vmem, smem] + [hbm] * 5,
            out_specs=(vmem, vmem, vmem),
            scratch_shapes=[
                pltpu.VMEM((256, leaf_cols), BF16),
                pltpu.VMEM((height, leaf_cols), BF16),
                pltpu.VMEM((LANES, cols), BF16),
                pltpu.VMEM((LANES, cols), BF16),
                pltpu.VMEM((LANES, cols), BF16),
                pltpu.VMEM((LANES, height), BF16),
                pltpu.VMEM((LANES, LANES), BF16),
                pltpu.VMEM((32, leaf_cols), BF16),
                pltpu.VMEM((16 * n, height), BF16),
                pltpu.VMEM((16 * n, height), BF16),
                pltpu.VMEM((32, leaf_cols), F32),
            ]
            + [pltpu.VMEM(shape, kind) for shape, kind in buffers]
            + [
                pltpu.SemaphoreType.DMA((5,)),
                pltpu.SemaphoreType.DMA((PHASES,)),
                pltpu.SemaphoreType.DMA((PHASES,)),
            ],
            compiler_params=pltpu.CompilerParams(
                collective_id=0, has_side_effects=True, vmem_limit_bytes=48 << 20
            ),
            name="solve",
        )(
            leaf_rhs,
            parent_rhs[:, 0, :],
            root_rhs,
            leaf_rows,
            leaf_height,
            parent_rows,
            parent_height,
            leaf_inv.reshape(-1, leaf_cols),
            leaf_panel.reshape(-1, leaf_cols),
            parent_inv[0],
            parent_panel[0],
            root_inv,
        )
        leaf_sol = leaf_out.reshape(2, 8, 2, HALF).transpose(1, 0, 2, 3).reshape(8, 4, HALF)
        return leaf_sol, parent_out[:, None, :], root_out

    return jax.shard_map(
        shards,
        mesh=mesh,
        in_specs=(
            P(None, "leaf", "rows"),
            P(None, "leaf", "rows"),
            P(None, ("leaf", "rows")),
            P("leaf", "rows", None),
            P("leaf", "rows", None),
            P("leaf", "rows"),
            P("leaf"),
            P("leaf", "rows", None),
            P("leaf", "rows", None),
            P("leaf", "rows"),
            P("leaf"),
            P("rows", None),
        ),
        out_specs=(P(None, "leaf", "rows"), P(None, "leaf", "rows"), P(None, ("leaf", "rows"))),
        check_vma=False,
    )
```

```python
import functools

import jax
import jax.numpy as jnp
from jax import lax
from jax.experimental import pallas as pl
from jax.experimental.pallas import tpu as pltpu
from jax.sharding import PartitionSpec as P

F32 = jnp.float32
BF16 = jnp.bfloat16
LANES = 128
HALF = 64
NT = (((1,), (1,)), ((), ()))
PHASES = 15


def dot(a, b):
    return jnp.dot(a, b, preferred_element_type=F32)


def dot_nt(a, b):
    return lax.dot_general(a, b, NT, preferred_element_type=F32)


def swap_halves(x):
    return pltpu.roll(x, HALF, 1)


def kernel(
    n,
    groups,
    leaf_rhs_hbm,
    parent_rhs_hbm,
    root_rhs_hbm,
    leaf_rows_hbm,
    leaf_height_hbm,
    parent_rows_hbm,
    parent_height_hbm,
    leaf_inv_hbm,
    leaf_panel_hbm,
    parent_inv_hbm,
    parent_panel_hbm,
    root_inv_hbm,
    leaf_out,
    parent_out,
    root_out,
    leaf_rhs,
    parent_rhs,
    root_rhs,
    leaf_rows,
    leaf_height,
    parent_rows,
    parent_height,
    leaf_inv,
    leaf_panel,
    parent_inv,
    parent_panel,
    root_inv,
    onehot,
    onehot_p,
    xs,
    spread_hi,
    spread_lo,
    terms,
    g1,
    g2,
    s3,
    r3,
    g4,
    g5,
    s6,
    r6,
    g7a,
    g7b,
    s8,
    r8,
    g9,
    s10,
    r10,
    s11,
    r11,
    g12,
    s13,
    r13,
    s14,
    r14,
    load_sem,
    send_sem,
    recv_sem,
):
    group = lax.axis_index("leaf")
    me = lax.axis_index("rows")

    barrier = pltpu.get_barrier_semaphore()

    def peer_of(i):
        if n != 32:
            return lax.rem(me + i + 1, n)

        def far_first(a):
            high = lax.div(a, 2)
            return 2 * (1 - high) + lax.rem(high + a, 2)

        z = lax.rem(lax.div(me, 8) + far_first(lax.div(i, 8)), 4)
        x = lax.rem(lax.div(me, 2) + far_first(lax.rem(lax.div(i, 2), 4)), 4)
        return 8 * z + 2 * x + lax.rem(me + 1 - lax.rem(i, 2), 2)

    def greet_row(i, carry):
        pl.semaphore_signal(barrier, inc=1, device_id={"rows": peer_of(i)})
        return carry

    lax.fori_loop(0, n - 1, greet_row, 0)
    for i in range(1, groups):
        pl.semaphore_signal(barrier, inc=1, device_id={"leaf": lax.rem(group + i, groups)})

    loads = [
        pltpu.make_async_copy(src, dst, load_sem.at[i])
        for i, (src, dst) in enumerate(
            (
                (leaf_rhs_hbm, leaf_rhs),
                (leaf_rows_hbm, leaf_rows),
                (leaf_height_hbm, leaf_height),
                (parent_rows_hbm, parent_rows),
                (parent_height_hbm, parent_height),
                (root_rhs_hbm, root_rhs),
                (parent_rhs_hbm, parent_rhs),
                (leaf_inv_hbm, leaf_inv),
                (leaf_panel_hbm, leaf_panel),
                (parent_inv_hbm, parent_inv),
                (parent_panel_hbm, parent_panel),
                (root_inv_hbm, root_inv),
            )
        )
    ]
    for copy in loads:
        copy.start()

    low = lax.broadcasted_iota(jnp.int32, (8, LANES), 1) < HALF
    low16 = lax.broadcasted_iota(jnp.int32, (16, LANES), 1) < HALF

    def drain(ref, sem, count):
        view = ref.at[pl.ds(0, count)]
        pltpu.make_async_copy(view, view, sem).wait()

    def gather_start(ref, value, phase):
        ref[me] = value

        def send(i, carry):
            pltpu.make_async_remote_copy(
                src_ref=ref.at[me],
                dst_ref=ref.at[me],
                send_sem=send_sem.at[phase],
                recv_sem=recv_sem.at[phase],
                device_id={"rows": peer_of(i)},
            ).start()
            return carry

        lax.fori_loop(0, n - 1, send, 0)

    def gather_wait(ref, phase):
        drain(ref, recv_sem.at[phase], n - 1)

    def scatter_start(src, dst, phase):
        def send(i, carry):
            peer = peer_of(i)
            pltpu.make_async_remote_copy(
                src_ref=src.at[peer],
                dst_ref=dst.at[me],
                send_sem=send_sem.at[phase],
                recv_sem=recv_sem.at[phase],
                device_id={"rows": peer},
            ).start()
            return carry

        lax.fori_loop(0, n - 1, send, 0)
        dst[me] = src[me]

    def scatter_sum(dst, phase):
        drain(dst, recv_sem.at[phase], n - 1)
        return jnp.sum(dst[...].astype(F32), axis=0)

    def pack_rhs():
        tops = [
            jnp.concatenate([leaf_rhs[:, 2 * a, :], leaf_rhs[:, 2 * a + 1, :]], axis=1)
            for a in range(2)
        ]
        return jnp.concatenate(tops, axis=0).astype(BF16)

    def unpack(ref):
        for c in range(n // 2):
            even = ref[2 * c].astype(F32)
            odd = ref[2 * c + 1].astype(F32)
            cols = pl.ds(c * LANES, LANES)
            xs[0:16, cols] = jnp.where(low16, even, swap_halves(odd)).astype(BF16)
            xs[16:32, cols] = jnp.where(low16, swap_halves(even), odd).astype(BF16)

    def pack_terms(dst):
        for c in range(n // 2):
            cols = pl.ds(c * LANES, LANES)
            first, second = [], []
            for a in range(2):
                even = terms[pl.ds(16 * a, 8), cols]
                odd = terms[pl.ds(16 * a + 8, 8), cols]
                first.append(jnp.where(low, even, swap_halves(odd)))
                second.append(jnp.where(low, swap_halves(even), odd))
            dst[2 * c] = jnp.concatenate(first, axis=0).astype(BF16)
            dst[2 * c + 1] = jnp.concatenate(second, axis=0).astype(BF16)

    def columns(ref):
        return jnp.concatenate([ref[c] for c in range(n)], axis=1)

    def spread(value, where_at, blocks, width):
        high = value.astype(BF16).astype(F32)
        rest = value - high
        for q in range(0, blocks, 2):
            rows = pl.ds(8 * q, 16)
            for part, ref in ((high, spread_hi), (rest, spread_lo)):
                pair = [jnp.where(where_at == q + k, part, 0.0) for k in range(2)]
                ref[rows, 0:width] = jnp.concatenate(pair, axis=0).astype(BF16)

    def pick(table, where_at, first):
        total = jnp.zeros(where_at.shape, F32)
        for q in range(n):
            total += jnp.where(where_at == first + q, table[8 * q : 8 * q + 8, :], 0.0)
        return total

    loads[0].wait()
    packed_rhs = pack_rhs()
    pl.semaphore_wait(barrier, n - 1 + groups - 1)
    gather_start(g1, packed_rhs, 0)

    for copy in loads[1:7]:
        copy.wait()
    piece = leaf_rows.shape[1]
    at_list, low_list = [], []
    for s in range(4):
        rows_s = leaf_rows[s : s + 1, :]
        pos = me * piece + lax.broadcasted_iota(jnp.int32, (1, piece), 1)
        at_list.append(jnp.where(pos < leaf_height[s], rows_s >> 7, -1))
        low_list.append(rows_s & (LANES - 1))
    height = 4 * piece
    leaf_at = jnp.broadcast_to(jnp.concatenate(at_list, axis=1), (8, height))
    leaf_low = jnp.concatenate(low_list, axis=1)
    onehot[...] = jnp.where(
        lax.broadcasted_iota(jnp.int32, (LANES, height), 0) == leaf_low, 1.0, 0.0
    ).astype(BF16)
    rows_p = parent_rows[...]
    pos_p = me * LANES + lax.broadcasted_iota(jnp.int32, (1, LANES), 1)
    parent_at = jnp.broadcast_to(
        jnp.where(pos_p < parent_height[0], rows_p >> 7, -1), (8, LANES)
    )
    onehot_p[...] = jnp.where(
        lax.broadcasted_iota(jnp.int32, (LANES, LANES), 0) == (rows_p & (LANES - 1)), 1.0, 0.0
    ).astype(BF16)

    loads[7].wait()
    gather_wait(g1, 0)
    unpack(g1)
    full = dot_nt(xs[...], leaf_inv[...])
    ly = jnp.concatenate(
        [
            jnp.where(low, full[0:8, 0:LANES], full[16:24, 0:LANES]),
            jnp.where(low, full[8:16, LANES:], full[24:32, LANES:]),
        ],
        axis=0,
    )
    gather_start(g2, ly.astype(BF16), 1)
    loads[8].wait()
    gather_wait(g2, 1)
    unpack(g2)
    updates = []
    for s in range(4):
        a, b = s // 2, s % 2
        got = dot_nt(xs[16 * b : 16 * b + 16, :], leaf_panel[pl.ds(s * piece, piece), :])
        updates.append(got[8 * a : 8 * a + 8, :])
    spread(jnp.concatenate(updates, axis=1), leaf_at, 2 * n, height)
    acc = dot_nt(spread_hi[...], onehot[...]) + dot_nt(spread_lo[...], onehot[...])
    for q in range(2 * n):
        s3[q % n, q // n] = acc[8 * q : 8 * q + 8, :].astype(BF16)
    scatter_start(s3, r3, 2)
    sums = scatter_sum(r3, 2)

    prb = (parent_rhs[...] - sums[0]).astype(BF16)
    gather_start(g4, prb, 3)
    loads[9].wait()
    gather_wait(g4, 3)
    py = dot_nt(columns(g4), parent_inv[...])
    gather_start(g5, py.astype(BF16), 4)
    loads[10].wait()
    gather_wait(g5, 4)
    pupd = dot_nt(columns(g5), parent_panel[...])
    spread(pupd, parent_at, n, LANES)
    acc_p = dot_nt(spread_hi[0 : 8 * n, 0:LANES], onehot_p[...]) + dot_nt(
        spread_lo[0 : 8 * n, 0:LANES], onehot_p[...]
    )
    for q in range(n):
        s6[q] = acc_p[8 * q : 8 * q + 8, :]
    width = root_rhs.shape[1]
    per_slab = LANES // width
    slab = lax.div(group * n + me, per_slab)
    part = lax.rem(me, per_slab)
    lane_part = lax.broadcasted_iota(jnp.int32, (8, LANES), 1) // width
    mine = jnp.concatenate([root_rhs[...]] * per_slab, axis=1)
    s6[slab] = s6[slab] - jnp.where(lane_part == part, mine, 0.0)
    scatter_start(s6, r6, 5)
    partial = scatter_sum(r6, 5) + sums[1]

    g7a[group] = partial
    for i in range(1, groups):
        pltpu.make_async_remote_copy(
            src_ref=g7a.at[group],
            dst_ref=g7a.at[group],
            send_sem=send_sem.at[6],
            recv_sem=recv_sem.at[6],
            device_id={"leaf": lax.rem(group + i, groups)},
        ).start()
    drain(g7a, recv_sem.at[6], groups - 1)
    rrb = (-jnp.sum(g7a[...], axis=0)).astype(BF16)
    gather_start(g7b, rrb, 7)
    loads[11].wait()
    gather_wait(g7b, 7)
    ry = dot_nt(columns(g7b), root_inv[...])
    root_term = dot(ry.astype(BF16), root_inv[...])
    for c in range(n):
        s8[c] = root_term[:, c * LANES : (c + 1) * LANES]
    scatter_start(s8, r8, 8)
    root_slab = scatter_sum(r8, 8)
    gather_start(g9, root_slab.astype(BF16), 9)
    gather_wait(g9, 9)

    rxb = g9[...].reshape(n * 8, LANES)
    parent_anc = pick(dot(rxb, onehot_p[...]), parent_at, 0).astype(BF16)
    parent_term = dot(parent_anc, parent_panel[...])
    for c in range(n):
        s10[c] = parent_term[:, c * LANES : (c + 1) * LANES]
    scatter_start(s10, r10, 10)
    leaf_anc = pick(dot(rxb, onehot[...]), leaf_at, n)
    mine = jnp.where(lane_part == part, g9[slab].astype(F32), 0.0)
    root_out[...] = functools.reduce(
        lambda x, y: x + y, [mine[:, k * width : (k + 1) * width] for k in range(per_slab)]
    )
    pvb = (py - scatter_sum(r10, 10)).astype(BF16)
    parent_term = dot(pvb, parent_inv[...])
    for c in range(n):
        s11[c] = parent_term[:, c * LANES : (c + 1) * LANES]
    scatter_start(s11, r11, 11)
    parent_sol = scatter_sum(r11, 11)
    parent_out[...] = parent_sol
    gather_start(g12, parent_sol.astype(BF16), 12)
    gather_wait(g12, 12)

    pxb = g12[...].reshape(n * 8, LANES)
    leaf_anc = (leaf_anc + pick(dot(pxb, onehot[...]), leaf_at, 0)).astype(BF16)
    for s in range(4):
        terms[pl.ds(8 * s, 8), :] = dot(
            leaf_anc[:, s * piece : (s + 1) * piece], leaf_panel[pl.ds(s * piece, piece), :]
        )
    pack_terms(s13)
    scatter_start(s13, r13, 13)
    lvb = ly - scatter_sum(r13, 13)
    none = jnp.zeros((8, LANES), F32)
    blocks = []
    for s in range(4):
        a, b = s // 2, s % 2
        held = jnp.where(low if b == 0 else ~low, lvb[8 * a : 8 * a + 8, :], 0.0)
        blocks.append(jnp.concatenate([held, none] if a == 0 else [none, held], axis=1))
    terms[...] = dot(jnp.concatenate(blocks, axis=0).astype(BF16), leaf_inv[...])
    pack_terms(s14)
    scatter_start(s14, r14, 14)
    leaf_out[...] = scatter_sum(r14, 14)

    for phase, ref in enumerate(
        (g1, g2, r3, g4, g5, r6, g7a, g7b, r8, g9, r10, r11, g12, r13, r14)
    ):
        drain(ref, send_sem.at[phase], (groups if phase == 6 else n) - 1)


def solution(mesh):
    n = mesh.shape["rows"]
    groups = mesh.shape["leaf"]

    def shards(
        leaf_rhs,
        parent_rhs,
        root_rhs,
        leaf_inv,
        leaf_panel,
        leaf_rows,
        leaf_height,
        parent_inv,
        parent_panel,
        parent_rows,
        parent_height,
        root_inv,
    ):
        leaf_cols = leaf_inv.shape[2]
        cols = root_inv.shape[1]
        height = 4 * leaf_panel.shape[1]
        packed = (16, LANES)
        vmem = pl.BlockSpec(memory_space=pltpu.VMEM)
        hbm = pl.BlockSpec(memory_space=pl.ANY)
        slabs = (n, 8, LANES)
        buffers = [
            ((n, *packed), BF16),
            ((n, *packed), BF16),
            ((n, 2, 8, LANES), BF16),
            ((n, 2, 8, LANES), BF16),
            (slabs, BF16),
            (slabs, BF16),
            (slabs, F32),
            (slabs, F32),
            ((groups, 8, LANES), F32),
            (slabs, BF16),
            (slabs, F32),
            (slabs, F32),
            (slabs, BF16),
            (slabs, F32),
            (slabs, F32),
            (slabs, F32),
            (slabs, F32),
            (slabs, BF16),
            ((n, *packed), BF16),
            ((n, *packed), BF16),
            ((n, *packed), BF16),
            ((n, *packed), BF16),
        ]
        leaf_out, parent_out, root_out = pl.pallas_call(
            functools.partial(kernel, n, groups),
            out_shape=(
                jax.ShapeDtypeStruct(packed, F32),
                jax.ShapeDtypeStruct((8, LANES), F32),
                jax.ShapeDtypeStruct(root_rhs.shape, F32),
            ),
            in_specs=[hbm] * 12,
            out_specs=(vmem, vmem, vmem),
            scratch_shapes=[
                pltpu.VMEM(leaf_rhs.shape, F32),
                pltpu.VMEM((8, LANES), F32),
                pltpu.VMEM(root_rhs.shape, F32),
                pltpu.VMEM(leaf_rows.shape, jnp.int32),
                pltpu.SMEM(leaf_height.shape, jnp.int32),
                pltpu.VMEM(parent_rows.shape, jnp.int32),
                pltpu.SMEM(parent_height.shape, jnp.int32),
                pltpu.VMEM((256, leaf_cols), BF16),
                pltpu.VMEM((height, leaf_cols), BF16),
                pltpu.VMEM((LANES, cols), BF16),
                pltpu.VMEM((LANES, cols), BF16),
                pltpu.VMEM((LANES, cols), BF16),
                pltpu.VMEM((LANES, height), BF16),
                pltpu.VMEM((LANES, LANES), BF16),
                pltpu.VMEM((32, leaf_cols), BF16),
                pltpu.VMEM((16 * n, height), BF16),
                pltpu.VMEM((16 * n, height), BF16),
                pltpu.VMEM((32, leaf_cols), F32),
            ]
            + [pltpu.VMEM(shape, kind) for shape, kind in buffers]
            + [
                pltpu.SemaphoreType.DMA((12,)),
                pltpu.SemaphoreType.DMA((PHASES,)),
                pltpu.SemaphoreType.DMA((PHASES,)),
            ],
            compiler_params=pltpu.CompilerParams(
                collective_id=0, has_side_effects=True, vmem_limit_bytes=67043328
            ),
            name="solve",
        )(
            leaf_rhs,
            parent_rhs[:, 0, :],
            root_rhs,
            leaf_rows,
            leaf_height,
            parent_rows,
            parent_height,
            leaf_inv.reshape(-1, leaf_cols),
            leaf_panel.reshape(-1, leaf_cols),
            parent_inv[0],
            parent_panel[0],
            root_inv,
        )
        leaf_sol = leaf_out.reshape(2, 8, 2, HALF).transpose(1, 0, 2, 3).reshape(8, 4, HALF)
        return leaf_sol, parent_out[:, None, :], root_out

    return jax.shard_map(
        shards,
        mesh=mesh,
        in_specs=(
            P(None, "leaf", "rows"),
            P(None, "leaf", "rows"),
            P(None, ("leaf", "rows")),
            P("leaf", "rows", None),
            P("leaf", "rows", None),
            P("leaf", "rows"),
            P("leaf"),
            P("leaf", "rows", None),
            P("leaf", "rows", None),
            P("leaf", "rows"),
            P("leaf"),
            P("rows", None),
        ),
        out_specs=(P(None, "leaf", "rows"), P(None, "leaf", "rows"), P(None, ("leaf", "rows"))),
        check_vma=False,
    )
```

```python
import functools

import jax
import jax.numpy as jnp
from jax import lax
from jax.experimental import pallas as pl
from jax.experimental.pallas import tpu as pltpu
from jax.sharding import PartitionSpec as P

F32 = jnp.float32
BF16 = jnp.bfloat16
LANES = 128
HALF = 64
NT = (((1,), (1,)), ((), ()))
PHASES = 16
BULK = 15


def dot(a, b):
    return jnp.dot(a, b, preferred_element_type=F32)


def dot_nt(a, b):
    return lax.dot_general(a, b, NT, preferred_element_type=F32)


def swap_halves(x):
    return pltpu.roll(x, HALF, 1)


def kernel(
    n,
    groups,
    leaf_rhs_hbm,
    parent_rhs_hbm,
    root_rhs_hbm,
    leaf_rows_hbm,
    leaf_height_hbm,
    parent_rows_hbm,
    parent_height_hbm,
    leaf_inv_hbm,
    leaf_panel_hbm,
    parent_inv_hbm,
    parent_panel_hbm,
    root_inv_hbm,
    leaf_out,
    parent_out,
    root_out,
    leaf_rhs,
    parent_rhs,
    root_rhs,
    leaf_rows,
    leaf_height,
    parent_rows,
    parent_height,
    leaf_inv,
    leaf_panel,
    parent_inv,
    parent_panel,
    root_inv,
    panel_cols,
    all_rows,
    onehot,
    onehot_p,
    xs,
    spread_ref,
    spread_p,
    terms,
    g1,
    g2,
    s3p,
    r3p,
    s3r,
    r3r,
    g4,
    s6,
    r6,
    g7a,
    g7b,
    s8,
    r8,
    g9,
    s11,
    r11,
    g12,
    s13,
    r13,
    s14,
    r14,
    load_sem,
    send_sem,
    recv_sem,
):
    group = lax.axis_index("leaf")
    me = lax.axis_index("rows")

    barrier = pltpu.get_barrier_semaphore()

    if n == 32:
        z, x, core = lax.div(me, 8), lax.rem(lax.div(me, 2), 4), lax.rem(me, 2)
    order = [(x, c) for x in (2, 3, 1, 0) for c in (1, 0)]

    def each_peer(act):
        if n != 32:
            lax.fori_loop(1, n, lambda i, carry: (act(lax.rem(me + i, n)), carry)[1], 0)
            return

        def ring(i, carry):
            base = 8 * lax.rem(z + (2 + i) - 4 * lax.div(i, 2) + lax.div(i, 2), 4)
            for dx, dc in order:
                act(base + 2 * lax.rem(x + dx, 4) + lax.rem(core + dc, 2))
            return carry

        lax.fori_loop(0, 3, ring, 0)
        for dx, dc in order[:-1]:
            act(8 * z + 2 * lax.rem(x + dx, 4) + lax.rem(core + dc, 2))

    each_peer(lambda peer: pl.semaphore_signal(barrier, inc=1, device_id={"rows": peer}))
    for i in range(1, groups):
        pl.semaphore_signal(barrier, inc=1, device_id={"leaf": lax.rem(group + i, groups)})

    own_cols = parent_panel_hbm.at[:, pl.ds(pl.multiple_of(me * LANES, LANES), LANES)]
    loads = [
        pltpu.make_async_copy(src, dst, load_sem.at[i])
        for i, (src, dst) in enumerate(
            (
                (leaf_rhs_hbm, leaf_rhs),
                (leaf_rows_hbm, leaf_rows),
                (leaf_height_hbm, leaf_height),
                (parent_rows_hbm, parent_rows),
                (parent_height_hbm, parent_height),
                (root_rhs_hbm, root_rhs),
                (parent_rhs_hbm, parent_rhs),
                (leaf_inv_hbm, leaf_inv),
                (leaf_panel_hbm, leaf_panel),
                (parent_inv_hbm, parent_inv),
                (parent_panel_hbm, parent_panel),
                (root_inv_hbm, root_inv),
                (own_cols, panel_cols.at[me]),
            )
        )
    ]
    for copy in loads:
        copy.start()

    low = lax.broadcasted_iota(jnp.int32, (8, LANES), 1) < HALF
    low16 = lax.broadcasted_iota(jnp.int32, (16, LANES), 1) < HALF

    def drain(ref, sem, count):
        view = ref.at[pl.ds(0, count)]
        pltpu.make_async_copy(view, view, sem).wait()

    def gather_start(ref, value, phase):
        ref[me] = value
        each_peer(
            lambda peer: pltpu.make_async_remote_copy(
                src_ref=ref.at[me],
                dst_ref=ref.at[me],
                send_sem=send_sem.at[phase],
                recv_sem=recv_sem.at[phase],
                device_id={"rows": peer},
            ).start()
        )

    def gather_wait(ref, phase):
        drain(ref, recv_sem.at[phase], n - 1)

    def scatter_start(src, dst, phase):
        each_peer(
            lambda peer: pltpu.make_async_remote_copy(
                src_ref=src.at[peer],
                dst_ref=dst.at[me],
                send_sem=send_sem.at[phase],
                recv_sem=recv_sem.at[phase],
                device_id={"rows": peer},
            ).start()
        )
        dst[me] = src[me]

    def send_panel(first, last):
        def send(i, carry):
            peer = lax.rem(me + i, n)
            cols = pl.ds(pl.multiple_of(peer * LANES, LANES), LANES)
            pltpu.make_async_remote_copy(
                src_ref=parent_panel.at[:, cols],
                dst_ref=panel_cols.at[me],
                send_sem=send_sem.at[BULK],
                recv_sem=recv_sem.at[BULK],
                device_id={"rows": peer},
            ).start()
            return carry

        lax.fori_loop(first, last, send, 0)

    def scatter_sum(dst, phase):
        drain(dst, recv_sem.at[phase], n - 1)
        return jnp.sum(dst[...].astype(F32), axis=0)

    def pack_rhs():
        tops = [
            jnp.concatenate([leaf_rhs[:, 2 * a, :], leaf_rhs[:, 2 * a + 1, :]], axis=1)
            for a in range(2)
        ]
        return jnp.concatenate(tops, axis=0).astype(BF16)

    def unpack(ref):
        for c in range(n // 2):
            even = ref[2 * c].astype(F32)
            odd = ref[2 * c + 1].astype(F32)
            cols = pl.ds(c * LANES, LANES)
            xs[0:16, cols] = jnp.where(low16, even, swap_halves(odd)).astype(BF16)
            xs[16:32, cols] = jnp.where(low16, swap_halves(even), odd).astype(BF16)

    def pack_terms(dst):
        for c in range(n // 2):
            cols = pl.ds(c * LANES, LANES)
            first, second = [], []
            for a in range(2):
                even = terms[pl.ds(16 * a, 8), cols]
                odd = terms[pl.ds(16 * a + 8, 8), cols]
                first.append(jnp.where(low, even, swap_halves(odd)))
                second.append(jnp.where(low, swap_halves(even), odd))
            dst[2 * c] = jnp.concatenate(first, axis=0).astype(BF16)
            dst[2 * c + 1] = jnp.concatenate(second, axis=0).astype(BF16)

    def columns(ref):
        return jnp.concatenate([ref[c] for c in range(n)], axis=1)

    def spread(value, where_at, first, ref):
        pair = jnp.concatenate([value, value], axis=0).astype(BF16)
        second = lax.broadcasted_iota(jnp.int32, pair.shape, 0) >= 8
        at = jnp.concatenate([where_at, where_at], axis=0) - jnp.where(second, 1, 0)
        at = at.astype(F32).astype(BF16)
        for q in range(0, n, 2):
            number = jnp.array(first + q, BF16)
            ref[pl.ds(8 * q, 16), :] = jnp.where(at == number, pair, jnp.array(0.0, BF16))

    def pick(table, where_at, first):
        total = jnp.zeros(where_at.shape, F32)
        for q in range(n):
            total += jnp.where(where_at == first + q, table[8 * q : 8 * q + 8, :], 0.0)
        return total

    loads[0].wait()
    packed_rhs = pack_rhs()
    pl.semaphore_wait(barrier, n - 1 + groups - 1)
    gather_start(g1, packed_rhs, 0)
    for copy in loads[1:7]:
        copy.wait()
    all_rows[me] = parent_rows[...]
    each_peer(
        lambda peer: pltpu.make_async_remote_copy(
            src_ref=all_rows.at[me],
            dst_ref=all_rows.at[me],
            send_sem=send_sem.at[4],
            recv_sem=recv_sem.at[4],
            device_id={"rows": peer},
        ).start()
    )
    loads[10].wait()
    quarter = -(-(n - 1) // 4)
    send_panel(1, 1 + quarter)

    piece = leaf_rows.shape[1]
    at_list, low_list = [], []
    for s in range(4):
        rows_s = leaf_rows[s : s + 1, :]
        pos = me * piece + lax.broadcasted_iota(jnp.int32, (1, piece), 1)
        at_list.append(jnp.where(pos < leaf_height[s], rows_s >> 7, -1))
        low_list.append(rows_s & (LANES - 1))
    height = 4 * piece
    leaf_at = jnp.broadcast_to(jnp.concatenate(at_list, axis=1), (8, height))
    leaf_low = jnp.concatenate(low_list, axis=1)
    onehot[...] = jnp.where(
        lax.broadcasted_iota(jnp.int32, (LANES, height), 0) == leaf_low, 1.0, 0.0
    ).astype(BF16)

    loads[7].wait()
    gather_wait(g1, 0)
    unpack(g1)
    full = dot_nt(xs[...], leaf_inv[...])
    ly = jnp.concatenate(
        [
            jnp.where(low, full[0:8, 0:LANES], full[16:24, 0:LANES]),
            jnp.where(low, full[8:16, LANES:], full[24:32, LANES:]),
        ],
        axis=0,
    )
    gather_start(g2, ly.astype(BF16), 1)
    send_panel(1 + quarter, 1 + 2 * quarter)

    drain(all_rows, recv_sem.at[4], n - 1)
    rows_p = jnp.concatenate([all_rows[c] for c in range(n)], axis=1)
    pos_p = lax.broadcasted_iota(jnp.int32, rows_p.shape, 1)
    parent_at = jnp.broadcast_to(
        jnp.where(pos_p < parent_height[0], rows_p >> 7, -1), (8, n * LANES)
    )
    onehot_p[...] = jnp.where(
        lax.broadcasted_iota(jnp.int32, onehot_p.shape, 0) == (rows_p & (LANES - 1)), 1.0, 0.0
    ).astype(BF16)

    loads[8].wait()
    gather_wait(g2, 1)
    unpack(g2)
    updates = []
    for s in range(4):
        a, b = s // 2, s % 2
        got = dot_nt(xs[16 * b : 16 * b + 16, :], leaf_panel[pl.ds(s * piece, piece), :])
        updates.append(got[8 * a : 8 * a + 8, :])
    updates = jnp.concatenate(updates, axis=1)
    spread(updates, leaf_at, 0, spread_ref)
    s3p[...] = dot_nt(spread_ref[...], onehot[...]).astype(BF16).reshape(n, 8, LANES)
    scatter_start(s3p, r3p, 2)
    send_panel(1 + 2 * quarter, 1 + 3 * quarter)
    spread(updates, leaf_at, n, spread_ref)
    s3r[...] = dot_nt(spread_ref[...], onehot[...]).astype(BF16).reshape(n, 8, LANES)
    pacc = scatter_sum(r3p, 2)

    prb = (parent_rhs[...] - pacc).astype(BF16)
    gather_start(g4, prb, 3)
    scatter_start(s3r, r3r, 10)
    send_panel(1 + 3 * quarter, n)
    loads[9].wait()
    loads[12].wait()
    gather_wait(g4, 3)
    py = dot_nt(columns(g4), parent_inv[...])
    drain(panel_cols, recv_sem.at[BULK], n - 1)
    cols_of = panel_cols[...].reshape(n * LANES, LANES)
    spread(dot_nt(py.astype(BF16), cols_of), parent_at, 0, spread_p)
    s6[...] = dot_nt(spread_p[...], onehot_p[...]).reshape(n, 8, LANES)
    width = root_rhs.shape[1]
    per_slab = LANES // width
    slab = lax.div(group * n + me, per_slab)
    part = lax.rem(me, per_slab)
    lane_part = lax.broadcasted_iota(jnp.int32, (8, LANES), 1) // width
    mine = jnp.concatenate([root_rhs[...]] * per_slab, axis=1)
    s6[slab] = s6[slab] - jnp.where(lane_part == part, mine, 0.0)
    scatter_start(s6, r6, 5)
    racc = scatter_sum(r3r, 10)
    partial = scatter_sum(r6, 5) + racc

    g7a[group] = partial
    for i in range(1, groups):
        pltpu.make_async_remote_copy(
            src_ref=g7a.at[group],
            dst_ref=g7a.at[group],
            send_sem=send_sem.at[6],
            recv_sem=recv_sem.at[6],
            device_id={"leaf": lax.rem(group + i, groups)},
        ).start()
    drain(g7a, recv_sem.at[6], groups - 1)
    rrb = (-jnp.sum(g7a[...], axis=0)).astype(BF16)
    gather_start(g7b, rrb, 7)
    loads[11].wait()
    gather_wait(g7b, 7)
    ry = dot_nt(columns(g7b), root_inv[...])
    root_term = dot(ry.astype(BF16), root_inv[...])
    for c in range(n):
        s8[c] = root_term[:, c * LANES : (c + 1) * LANES]
    scatter_start(s8, r8, 8)
    root_slab = scatter_sum(r8, 8)
    gather_start(g9, root_slab.astype(BF16), 9)
    gather_wait(g9, 9)

    rxb = g9[...].reshape(n * 8, LANES)
    pt = jnp.zeros((8, LANES), F32)
    chunk = 4 * LANES
    for c in range(0, n * LANES, chunk):
        cols = slice(c, c + chunk)
        got = pick(dot(rxb, onehot_p[:, cols]), parent_at[:, cols], 0).astype(BF16)
        pt += dot(got, panel_cols[c // LANES : (c + chunk) // LANES].reshape(chunk, LANES))
    pvb = (py - pt).astype(BF16)
    parent_term = dot(pvb, parent_inv[...])
    for c in range(n):
        s11[c] = parent_term[:, c * LANES : (c + 1) * LANES]
    scatter_start(s11, r11, 11)
    root_anc = [
        pick(
            dot(rxb, onehot[:, s * piece : (s + 1) * piece]),
            leaf_at[:, s * piece : (s + 1) * piece],
            n,
        )
        for s in range(4)
    ]
    mine = jnp.where(lane_part == part, g9[slab].astype(F32), 0.0)
    root_out[...] = functools.reduce(
        lambda x, y: x + y, [mine[:, k * width : (k + 1) * width] for k in range(per_slab)]
    )
    parent_sol = scatter_sum(r11, 11)
    gather_start(g12, parent_sol.astype(BF16), 12)
    parent_out[...] = parent_sol
    gather_wait(g12, 12)

    pxb = g12[...].reshape(n * 8, LANES)
    for s in range(4):
        cols = slice(s * piece, (s + 1) * piece)
        got = (root_anc[s] + pick(dot(pxb, onehot[:, cols]), leaf_at[:, cols], 0)).astype(BF16)
        terms[pl.ds(8 * s, 8), :] = dot(got, leaf_panel[pl.ds(s * piece, piece), :])
    pack_terms(s13)
    scatter_start(s13, r13, 13)
    lvb = ly - scatter_sum(r13, 13)
    none = jnp.zeros((8, LANES), F32)
    blocks = []
    for s in range(4):
        a, b = s // 2, s % 2
        held = jnp.where(low if b == 0 else ~low, lvb[8 * a : 8 * a + 8, :], 0.0)
        blocks.append(jnp.concatenate([held, none] if a == 0 else [none, held], axis=1))
    terms[...] = dot(jnp.concatenate(blocks, axis=0).astype(BF16), leaf_inv[...])
    pack_terms(s14)
    scatter_start(s14, r14, 14)
    result = scatter_sum(r14, 14)
    for a in range(2):
        rows = result[8 * a : 8 * a + 8, :]
        leaf_out[:, 2 * a, :] = rows[:, :HALF]
        leaf_out[:, 2 * a + 1, :] = swap_halves(rows)[:, :HALF]

    for phase, ref in enumerate(
        (g1, g2, r3p, g4, all_rows, r6, g7a, g7b, r8, g9, r3r, r11, g12, r13, r14, panel_cols)
    ):
        drain(ref, send_sem.at[phase], (groups if phase == 6 else n) - 1)


def store(count, *refs):
    copies = [
        pltpu.make_async_copy(refs[i], refs[count + i], refs[-1].at[i]) for i in range(count)
    ]
    for copy in copies:
        copy.start()
    for copy in copies:
        copy.wait()


def solution(mesh):
    n = mesh.shape["rows"]
    groups = mesh.shape["leaf"]

    def shards(
        leaf_rhs,
        parent_rhs,
        root_rhs,
        leaf_inv,
        leaf_panel,
        leaf_rows,
        leaf_height,
        parent_inv,
        parent_panel,
        parent_rows,
        parent_height,
        root_inv,
    ):
        leaf_cols = leaf_inv.shape[2]
        cols = root_inv.shape[1]
        height = 4 * leaf_panel.shape[1]
        packed = (16, LANES)
        vmem = pl.BlockSpec(memory_space=pltpu.VMEM)
        hbm = pl.BlockSpec(memory_space=pltpu.HBM)
        slabs = (n, 8, LANES)
        buffers = [
            ((n, *packed), BF16),
            ((n, *packed), BF16),
            (slabs, BF16),
            (slabs, BF16),
            (slabs, BF16),
            (slabs, BF16),
            (slabs, BF16),
            (slabs, F32),
            (slabs, F32),
            ((groups, 8, LANES), F32),
            (slabs, BF16),
            (slabs, F32),
            (slabs, F32),
            (slabs, BF16),
            (slabs, F32),
            (slabs, F32),
            (slabs, BF16),
            ((n, *packed), BF16),
            ((n, *packed), BF16),
            ((n, *packed), BF16),
            ((n, *packed), BF16),
        ]
        leaf_out, parent_out, root_out = pl.pallas_call(
            functools.partial(kernel, n, groups),
            out_shape=(
                jax.ShapeDtypeStruct((8, 4, HALF), F32),
                jax.ShapeDtypeStruct((8, LANES), F32),
                jax.ShapeDtypeStruct(root_rhs.shape, F32),
            ),
            in_specs=[hbm] * 12,
            out_specs=(vmem, vmem, vmem),
            scratch_shapes=[
                pltpu.VMEM(leaf_rhs.shape, F32),
                pltpu.VMEM((8, LANES), F32),
                pltpu.VMEM(root_rhs.shape, F32),
                pltpu.VMEM(leaf_rows.shape, jnp.int32),
                pltpu.SMEM(leaf_height.shape, jnp.int32),
                pltpu.VMEM(parent_rows.shape, jnp.int32),
                pltpu.SMEM(parent_height.shape, jnp.int32),
                pltpu.VMEM((256, leaf_cols), BF16),
                pltpu.VMEM((height, leaf_cols), BF16),
                pltpu.VMEM((LANES, cols), BF16),
                pltpu.VMEM((LANES, cols), BF16),
                pltpu.VMEM((LANES, cols), BF16),
                pltpu.VMEM((n, LANES, LANES), BF16),
                pltpu.VMEM((n, 1, LANES), jnp.int32),
                pltpu.VMEM((LANES, height), BF16),
                pltpu.VMEM((LANES, cols), BF16),
                pltpu.VMEM((32, leaf_cols), BF16),
                pltpu.VMEM((8 * n, height), BF16),
                pltpu.VMEM((8 * n, cols), BF16),
                pltpu.VMEM((32, leaf_cols), F32),
            ]
            + [pltpu.VMEM(shape, kind) for shape, kind in buffers]
            + [
                pltpu.SemaphoreType.DMA((13,)),
                pltpu.SemaphoreType.DMA((PHASES,)),
                pltpu.SemaphoreType.DMA((PHASES,)),
            ],
            compiler_params=pltpu.CompilerParams(
                collective_id=0, has_side_effects=True, vmem_limit_bytes=48 << 20
            ),
            name="solve",
        )(
            *(
                x if x.size == 1 else pltpu.with_memory_space_constraint(x, pltpu.HBM)
                for x in (
                    leaf_rhs,
                    parent_rhs[:, 0, :],
                    root_rhs,
                    leaf_rows,
                    leaf_height,
                    parent_rows,
                    parent_height,
                    leaf_inv.reshape(-1, leaf_cols),
                    leaf_panel.reshape(-1, leaf_cols),
                    parent_inv[0],
                    parent_panel[0],
                    root_inv,
                )
            )
        )
        results = (leaf_out, parent_out, root_out)
        leaf_out, parent_out, root_out = pl.pallas_call(
            functools.partial(store, 3),
            out_shape=tuple(jax.ShapeDtypeStruct(r.shape, r.dtype) for r in results),
            in_specs=[vmem] * 3,
            out_specs=(hbm,) * 3,
            scratch_shapes=[pltpu.SemaphoreType.DMA((3,))],
            name="store",
        )(*(pltpu.with_memory_space_constraint(r, pltpu.VMEM) for r in results))
        return leaf_out, parent_out[:, None, :], root_out

    return jax.shard_map(
        shards,
        mesh=mesh,
        in_specs=(
            P(None, "leaf", "rows"),
            P(None, "leaf", "rows"),
            P(None, ("leaf", "rows")),
            P("leaf", "rows", None),
            P("leaf", "rows", None),
            P("leaf", "rows"),
            P("leaf"),
            P("leaf", "rows", None),
            P("leaf", "rows", None),
            P("leaf", "rows"),
            P("leaf"),
            P("rows", None),
        ),
        out_specs=(P(None, "leaf", "rows"), P(None, "leaf", "rows"), P(None, ("leaf", "rows"))),
        check_vma=False,
    )
```

```python
import functools

import jax
import jax.numpy as jnp
from jax import lax
from jax.experimental import pallas as pl
from jax.experimental.pallas import tpu as pltpu
from jax.sharding import PartitionSpec as P

F32 = jnp.float32
BF16 = jnp.bfloat16
LANES = 128
HALF = 64
WIDE = 256
NT = (((1,), (1,)), ((), ()))
PHASES = 16
BULK = 15


def dot(a, b):
    return jnp.dot(a, b, preferred_element_type=F32)


def dot_nt(a, b):
    return lax.dot_general(a, b, NT, preferred_element_type=F32)


def swap_halves(x):
    return pltpu.roll(x, HALF, 1)


def kernel(
    n,
    groups,
    leaf_rhs_hbm,
    parent_rhs_hbm,
    root_rhs_hbm,
    leaf_rows_hbm,
    leaf_height_hbm,
    parent_rows_hbm,
    parent_height_hbm,
    leaf_inv_hbm,
    leaf_panel_hbm,
    parent_inv_hbm,
    parent_panel_hbm,
    root_inv_hbm,
    leaf_out,
    parent_out,
    root_out,
    leaf_rhs,
    parent_rhs,
    root_rhs,
    leaf_rows,
    leaf_height,
    parent_rows,
    parent_height,
    leaf_inv,
    leaf_panel,
    parent_inv,
    parent_panel,
    root_inv,
    panel_cols,
    all_rows,
    onehot,
    onehot_p,
    xs,
    panel_root,
    terms,
    g1,
    g2,
    s3p,
    r3p,
    s3r,
    r3r,
    g4,
    s6,
    r6,
    g7a,
    g7b,
    s8,
    r8,
    g9,
    s11,
    r11,
    g12,
    s13,
    r13,
    s14,
    r14,
    load_sem,
    send_sem,
    recv_sem,
):
    group = lax.axis_index("leaf")
    me = lax.axis_index("rows")

    barrier = pltpu.get_barrier_semaphore()

    if n == 32:
        z, x, core = lax.div(me, 8), lax.rem(lax.div(me, 2), 4), lax.rem(me, 2)
    order = [(x, c) for x in (2, 3, 1, 0) for c in (1, 0)]

    def each_peer(act):
        if n != 32:
            lax.fori_loop(1, n, lambda i, carry: (act(lax.rem(me + i, n)), carry)[1], 0)
            return

        def ring(i, carry):
            base = 8 * lax.rem(z + (2 + i) - 4 * lax.div(i, 2) + lax.div(i, 2), 4)
            for dx, dc in order:
                act(base + 2 * lax.rem(x + dx, 4) + lax.rem(core + dc, 2))
            return carry

        lax.fori_loop(0, 3, ring, 0)
        for dx, dc in order[:-1]:
            act(8 * z + 2 * lax.rem(x + dx, 4) + lax.rem(core + dc, 2))

    each_peer(lambda peer: pl.semaphore_signal(barrier, inc=1, device_id={"rows": peer}))
    for i in range(1, groups):
        pl.semaphore_signal(barrier, inc=1, device_id={"leaf": lax.rem(group + i, groups)})

    own_cols = parent_panel_hbm.at[:, pl.ds(pl.multiple_of(me * LANES, LANES), LANES)]
    loads = [
        pltpu.make_async_copy(src, dst, load_sem.at[i])
        for i, (src, dst) in enumerate(
            (
                (leaf_rhs_hbm, leaf_rhs),
                (leaf_rows_hbm, leaf_rows),
                (leaf_height_hbm, leaf_height),
                (parent_rows_hbm, parent_rows),
                (parent_height_hbm, parent_height),
                (root_rhs_hbm, root_rhs),
                (parent_rhs_hbm, parent_rhs),
                (leaf_inv_hbm, leaf_inv),
                (leaf_panel_hbm, leaf_panel),
                (parent_inv_hbm, parent_inv),
                (root_inv_hbm, root_inv),
                (own_cols, panel_cols.at[me]),
            )
        )
    ]
    for copy in loads:
        copy.start()

    def load_cols(c, carry):
        cols = pl.ds(pl.multiple_of(c * LANES, LANES), LANES)
        pltpu.make_async_copy(
            parent_panel_hbm.at[:, cols], parent_panel.at[c], load_sem.at[12]
        ).start()
        return carry

    lax.fori_loop(0, n, load_cols, 0)

    low = lax.broadcasted_iota(jnp.int32, (8, LANES), 1) < HALF
    low16 = lax.broadcasted_iota(jnp.int32, (16, LANES), 1) < HALF

    def drain(ref, sem, count):
        view = ref.at[pl.ds(0, count)]
        pltpu.make_async_copy(view, view, sem).wait()

    def gather_start(ref, value, phase):
        ref[me] = value
        each_peer(
            lambda peer: pltpu.make_async_remote_copy(
                src_ref=ref.at[me],
                dst_ref=ref.at[me],
                send_sem=send_sem.at[phase],
                recv_sem=recv_sem.at[phase],
                device_id={"rows": peer},
            ).start()
        )

    def gather_wait(ref, phase):
        drain(ref, recv_sem.at[phase], n - 1)

    def scatter_start(src, dst, phase):
        each_peer(
            lambda peer: pltpu.make_async_remote_copy(
                src_ref=src.at[peer],
                dst_ref=dst.at[me],
                send_sem=send_sem.at[phase],
                recv_sem=recv_sem.at[phase],
                device_id={"rows": peer},
            ).start()
        )
        dst[me] = src[me]

    def send_panel(turn):
        def send(i, carry):
            if n == 32:
                dz, dc = lax.div(i, 2), lax.rem(i, 2)
                dx = lax.rem(turn + 4 - dz, 4)
                row = 8 * lax.rem(z + dz, 4) + 2 * lax.rem(x + dx, 4)
                peer = row + lax.rem(core + dc, 2)
            else:
                peer = lax.rem(me + turn * n // 4 + i, n)
            pltpu.make_async_remote_copy(
                src_ref=parent_panel.at[peer],
                dst_ref=panel_cols.at[me],
                send_sem=send_sem.at[BULK],
                recv_sem=recv_sem.at[BULK],
                device_id={"rows": peer},
            ).start()
            return carry

        lax.fori_loop(0 if turn else 1, n // 4, send, 0)

    def scatter_sum(dst, phase):
        drain(dst, recv_sem.at[phase], n - 1)
        return jnp.sum(dst[...].astype(F32), axis=0)

    def pack_rhs():
        tops = [
            jnp.concatenate([leaf_rhs[:, 2 * a, :], leaf_rhs[:, 2 * a + 1, :]], axis=1)
            for a in range(2)
        ]
        return jnp.concatenate(tops, axis=0).astype(BF16)

    def unpack(ref):
        for c in range(n // 2):
            even = ref[2 * c].astype(F32)
            odd = ref[2 * c + 1].astype(F32)
            cols = pl.ds(c * LANES, LANES)
            xs[0:16, cols] = jnp.where(low16, even, swap_halves(odd)).astype(BF16)
            xs[16:32, cols] = jnp.where(low16, swap_halves(even), odd).astype(BF16)

    def pack_terms(dst):
        for c in range(n // 2):
            cols = pl.ds(c * LANES, LANES)
            first, second = [], []
            for a in range(2):
                even = terms[pl.ds(16 * a, 8), cols]
                odd = terms[pl.ds(16 * a + 8, 8), cols]
                first.append(jnp.where(low, even, swap_halves(odd)))
                second.append(jnp.where(low, swap_halves(even), odd))
            dst[2 * c] = jnp.concatenate(first, axis=0).astype(BF16)
            dst[2 * c + 1] = jnp.concatenate(second, axis=0).astype(BF16)

    def columns(ref):
        return jnp.concatenate([ref[c] for c in range(n)], axis=1)

    blocks = n // 2

    def spread(value, where_at, first):
        pair = jnp.concatenate([value, value], axis=0).astype(BF16)
        second = lax.broadcasted_iota(jnp.int32, pair.shape, 0) >= 8
        at = jnp.concatenate([where_at, where_at], axis=0) - jnp.where(second, 1, 0)
        at = at.astype(F32).astype(BF16)
        return jnp.concatenate(
            [
                jnp.where(at == jnp.array(first + q, BF16), pair, jnp.array(0.0, BF16))
                for q in range(0, blocks, 2)
            ],
            axis=0,
        )

    def put_blocks(dst, acc):
        for c in range(n):
            part = acc[8 * (c // 2) : 8 * (c // 2) + 8, LANES * (c % 2) : LANES * (c % 2 + 1)]
            dst[c] = part.astype(dst.dtype)

    def get_blocks(ref):
        return jnp.concatenate(
            [jnp.concatenate([ref[2 * q], ref[2 * q + 1]], axis=1) for q in range(blocks)], axis=0
        )

    def pick(table, where_at, first):
        total = jnp.zeros(where_at.shape, F32)
        for q in range(blocks):
            total += jnp.where(where_at == first + q, table[8 * q : 8 * q + 8, :], 0.0)
        return total

    def root_order(first, last):
        at = jnp.broadcast_to(parent_at[0:1, :], (16, n * LANES)).astype(F32).astype(BF16)
        for q in range(first, last):
            mine = at == jnp.array(q, BF16)
            chosen = jnp.concatenate(
                [
                    jnp.where(mine, onehot_p[16 * i : 16 * i + 16, :], jnp.array(0.0, BF16))
                    for i in range(WIDE // 16)
                ],
                axis=0,
            )
            panel_root[pl.ds(q * WIDE, WIDE), :] = dot(chosen, cols_of).astype(BF16)

    loads[0].wait()
    packed_rhs = pack_rhs()
    pl.semaphore_wait(barrier, n - 1 + groups - 1)
    gather_start(g1, packed_rhs, 0)
    for copy in loads[1:7]:
        copy.wait()
    all_rows[me] = parent_rows[...]
    each_peer(
        lambda peer: pltpu.make_async_remote_copy(
            src_ref=all_rows.at[me],
            dst_ref=all_rows.at[me],
            send_sem=send_sem.at[4],
            recv_sem=recv_sem.at[4],
            device_id={"rows": peer},
        ).start()
    )
    pltpu.make_async_copy(parent_panel, parent_panel, load_sem.at[12]).wait()
    send_panel(2)

    piece = leaf_rows.shape[1]
    at_list, low_list = [], []
    for s in range(4):
        rows_s = leaf_rows[s : s + 1, :]
        pos = me * piece + lax.broadcasted_iota(jnp.int32, (1, piece), 1)
        at_list.append(jnp.where(pos < leaf_height[s], rows_s >> 8, -1))
        low_list.append(rows_s & (WIDE - 1))
    height = 4 * piece
    leaf_at = jnp.broadcast_to(jnp.concatenate(at_list, axis=1), (8, height))
    leaf_low = jnp.concatenate(low_list, axis=1)
    onehot[...] = jnp.where(
        lax.broadcasted_iota(jnp.int32, (WIDE, height), 0) == leaf_low, 1.0, 0.0
    ).astype(BF16)

    loads[7].wait()
    gather_wait(g1, 0)
    unpack(g1)
    full = dot_nt(xs[...], leaf_inv[...])
    ly = jnp.concatenate(
        [
            jnp.where(low, full[0:8, 0:LANES], full[16:24, 0:LANES]),
            jnp.where(low, full[8:16, LANES:], full[24:32, LANES:]),
        ],
        axis=0,
    )
    gather_start(g2, ly.astype(BF16), 1)
    send_panel(1)

    drain(all_rows, recv_sem.at[4], n - 1)
    rows_p = jnp.concatenate([all_rows[c] for c in range(n)], axis=1)
    pos_p = lax.broadcasted_iota(jnp.int32, rows_p.shape, 1)
    parent_at = jnp.broadcast_to(
        jnp.where(pos_p < parent_height[0], rows_p >> 8, -1), (8, n * LANES)
    )
    onehot_p[...] = jnp.where(
        lax.broadcasted_iota(jnp.int32, onehot_p.shape, 0) == (rows_p & (WIDE - 1)), 1.0, 0.0
    ).astype(BF16)

    loads[8].wait()
    gather_wait(g2, 1)
    unpack(g2)
    updates = []
    acc = jnp.zeros((8 * blocks, WIDE), F32)
    for s in range(4):
        a, b = s // 2, s % 2
        cols = slice(s * piece, (s + 1) * piece)
        got = dot_nt(xs[16 * b : 16 * b + 16, :], leaf_panel[cols, :])
        updates.append(got[8 * a : 8 * a + 8, :])
        acc += dot_nt(spread(updates[s], leaf_at[:, cols], 0), onehot[:, cols])
    put_blocks(s3p, acc)
    scatter_start(s3p, r3p, 2)
    send_panel(3)
    acc = jnp.zeros((8 * blocks, WIDE), F32)
    for s in range(4):
        cols = slice(s * piece, (s + 1) * piece)
        acc += dot_nt(spread(updates[s], leaf_at[:, cols], blocks), onehot[:, cols])
    put_blocks(s3r, acc)
    pacc = scatter_sum(r3p, 2)

    prb = (parent_rhs[...] - pacc).astype(BF16)
    gather_start(g4, prb, 3)
    scatter_start(s3r, r3r, 10)
    send_panel(0)
    loads[9].wait()
    loads[11].wait()
    gather_wait(g4, 3)
    py = dot_nt(columns(g4), parent_inv[...])
    drain(panel_cols, recv_sem.at[BULK], n - 1)
    cols_of = panel_cols[...].reshape(n * LANES, LANES)
    pyb = py.astype(BF16)
    acc = jnp.zeros((8 * blocks, WIDE), F32)
    chunk = 4 * LANES
    for c in range(0, n * LANES, chunk):
        cols = slice(c, c + chunk)
        got = dot_nt(pyb, cols_of[cols, :])
        acc += dot_nt(spread(got, parent_at[:, cols], 0), onehot_p[:, cols])
    put_blocks(s6, acc)
    width = root_rhs.shape[1]
    per_slab = LANES // width
    slab = lax.div(group * n + me, per_slab)
    part = lax.rem(me, per_slab)
    lane_part = lax.broadcasted_iota(jnp.int32, (8, LANES), 1) // width
    mine = jnp.concatenate([root_rhs[...]] * per_slab, axis=1)
    s6[slab] = s6[slab] - jnp.where(lane_part == part, mine, 0.0)
    scatter_start(s6, r6, 5)
    root_order(0, (2 * blocks) // 8)
    racc = scatter_sum(r3r, 10)
    partial = scatter_sum(r6, 5) + racc

    g7a[group] = partial
    for i in range(1, groups):
        pltpu.make_async_remote_copy(
            src_ref=g7a.at[group],
            dst_ref=g7a.at[group],
            send_sem=send_sem.at[6],
            recv_sem=recv_sem.at[6],
            device_id={"leaf": lax.rem(group + i, groups)},
        ).start()
    root_order((2 * blocks) // 8, (3 * blocks) // 8)
    drain(g7a, recv_sem.at[6], groups - 1)
    rrb = (-jnp.sum(g7a[...], axis=0)).astype(BF16)
    gather_start(g7b, rrb, 7)
    root_order((3 * blocks) // 8, (5 * blocks) // 8)
    loads[10].wait()
    gather_wait(g7b, 7)
    ry = dot_nt(columns(g7b), root_inv[...])
    root_term = dot(ry.astype(BF16), root_inv[...])
    for c in range(n):
        s8[c] = root_term[:, c * LANES : (c + 1) * LANES]
    scatter_start(s8, r8, 8)
    root_order((5 * blocks) // 8, (7 * blocks) // 8)
    root_slab = scatter_sum(r8, 8)
    gather_start(g9, root_slab.astype(BF16), 9)
    root_order((7 * blocks) // 8, blocks)
    gather_wait(g9, 9)

    pt = dot(columns(g9), panel_root[...])
    pvb = (py - pt).astype(BF16)
    parent_term = dot(pvb, parent_inv[...])
    for c in range(n):
        s11[c] = parent_term[:, c * LANES : (c + 1) * LANES]
    scatter_start(s11, r11, 11)
    rxb = get_blocks(g9)
    root_anc = [
        pick(
            dot(rxb, onehot[:, s * piece : (s + 1) * piece]),
            leaf_at[:, s * piece : (s + 1) * piece],
            blocks,
        )
        for s in range(4)
    ]
    mine = jnp.where(lane_part == part, g9[slab].astype(F32), 0.0)
    root_out[...] = functools.reduce(
        lambda x, y: x + y, [mine[:, k * width : (k + 1) * width] for k in range(per_slab)]
    )
    parent_sol = scatter_sum(r11, 11)
    gather_start(g12, parent_sol.astype(BF16), 12)
    parent_out[...] = parent_sol
    gather_wait(g12, 12)

    pxb = get_blocks(g12)
    for s in range(4):
        cols = slice(s * piece, (s + 1) * piece)
        got = (root_anc[s] + pick(dot(pxb, onehot[:, cols]), leaf_at[:, cols], 0)).astype(BF16)
        terms[pl.ds(8 * s, 8), :] = dot(got, leaf_panel[pl.ds(s * piece, piece), :])
    pack_terms(s13)
    scatter_start(s13, r13, 13)
    lvb = ly - scatter_sum(r13, 13)
    none = jnp.zeros((8, LANES), F32)
    rows_of = []
    for s in range(4):
        a, b = s // 2, s % 2
        held = jnp.where(low if b == 0 else ~low, lvb[8 * a : 8 * a + 8, :], 0.0)
        rows_of.append(jnp.concatenate([held, none] if a == 0 else [none, held], axis=1))
    terms[...] = dot(jnp.concatenate(rows_of, axis=0).astype(BF16), leaf_inv[...])
    pack_terms(s14)
    scatter_start(s14, r14, 14)
    result = scatter_sum(r14, 14)
    for a in range(2):
        rows = result[8 * a : 8 * a + 8, :]
        leaf_out[:, 2 * a, :] = rows[:, :HALF]
        leaf_out[:, 2 * a + 1, :] = swap_halves(rows)[:, :HALF]

    for phase, ref in enumerate(
        (g1, g2, r3p, g4, all_rows, r6, g7a, g7b, r8, g9, r3r, r11, g12, r13, r14, panel_cols)
    ):
        drain(ref, send_sem.at[phase], (groups if phase == 6 else n) - 1)


def store(count, *refs):
    copies = [
        pltpu.make_async_copy(refs[i], refs[count + i], refs[-1].at[i]) for i in range(count)
    ]
    for copy in copies:
        copy.start()
    for copy in copies:
        copy.wait()


def solution(mesh):
    n = mesh.shape["rows"]
    groups = mesh.shape["leaf"]

    def shards(
        leaf_rhs,
        parent_rhs,
        root_rhs,
        leaf_inv,
        leaf_panel,
        leaf_rows,
        leaf_height,
        parent_inv,
        parent_panel,
        parent_rows,
        parent_height,
        root_inv,
    ):
        leaf_cols = leaf_inv.shape[2]
        cols = root_inv.shape[1]
        height = 4 * leaf_panel.shape[1]
        packed = (16, LANES)
        vmem = pl.BlockSpec(memory_space=pltpu.VMEM)
        hbm = pl.BlockSpec(memory_space=pltpu.HBM)
        slabs = (n, 8, LANES)
        buffers = [
            ((n, *packed), BF16),
            ((n, *packed), BF16),
            (slabs, BF16),
            (slabs, BF16),
            (slabs, BF16),
            (slabs, BF16),
            (slabs, BF16),
            (slabs, F32),
            (slabs, F32),
            ((groups, 8, LANES), F32),
            (slabs, BF16),
            (slabs, F32),
            (slabs, F32),
            (slabs, BF16),
            (slabs, F32),
            (slabs, F32),
            (slabs, BF16),
            ((n, *packed), BF16),
            ((n, *packed), BF16),
            ((n, *packed), BF16),
            ((n, *packed), BF16),
        ]
        leaf_out, parent_out, root_out = pl.pallas_call(
            functools.partial(kernel, n, groups),
            out_shape=(
                jax.ShapeDtypeStruct((8, 4, HALF), F32),
                jax.ShapeDtypeStruct((8, LANES), F32),
                jax.ShapeDtypeStruct(root_rhs.shape, F32),
            ),
            in_specs=[hbm] * 12,
            out_specs=(vmem, vmem, vmem),
            scratch_shapes=[
                pltpu.VMEM(leaf_rhs.shape, F32),
                pltpu.VMEM((8, LANES), F32),
                pltpu.VMEM(root_rhs.shape, F32),
                pltpu.VMEM(leaf_rows.shape, jnp.int32),
                pltpu.SMEM(leaf_height.shape, jnp.int32),
                pltpu.VMEM(parent_rows.shape, jnp.int32),
                pltpu.SMEM(parent_height.shape, jnp.int32),
                pltpu.VMEM((256, leaf_cols), BF16),
                pltpu.VMEM((height, leaf_cols), BF16),
                pltpu.VMEM((LANES, cols), BF16),
                pltpu.VMEM((n, LANES, LANES), BF16),
                pltpu.VMEM((LANES, cols), BF16),
                pltpu.VMEM((n, LANES, LANES), BF16),
                pltpu.VMEM((n, 1, LANES), jnp.int32),
                pltpu.VMEM((WIDE, height), BF16),
                pltpu.VMEM((WIDE, cols), BF16),
                pltpu.VMEM((32, leaf_cols), BF16),
                pltpu.VMEM((cols, LANES), BF16),
                pltpu.VMEM((32, leaf_cols), F32),
            ]
            + [pltpu.VMEM(shape, kind) for shape, kind in buffers]
            + [
                pltpu.SemaphoreType.DMA((13,)),
                pltpu.SemaphoreType.DMA((PHASES,)),
                pltpu.SemaphoreType.DMA((PHASES,)),
            ],
            compiler_params=pltpu.CompilerParams(
                collective_id=0, has_side_effects=True, vmem_limit_bytes=48 << 20
            ),
            name="solve",
        )(
            *(
                x if x.size == 1 else pltpu.with_memory_space_constraint(x, pltpu.HBM)
                for x in (
                    leaf_rhs,
                    parent_rhs[:, 0, :],
                    root_rhs,
                    leaf_rows,
                    leaf_height,
                    parent_rows,
                    parent_height,
                    leaf_inv.reshape(-1, leaf_cols),
                    leaf_panel.reshape(-1, leaf_cols),
                    parent_inv[0],
                    parent_panel[0],
                    root_inv,
                )
            )
        )
        results = (leaf_out, parent_out, root_out)
        leaf_out, parent_out, root_out = pl.pallas_call(
            functools.partial(store, 3),
            out_shape=tuple(jax.ShapeDtypeStruct(r.shape, r.dtype) for r in results),
            in_specs=[vmem] * 3,
            out_specs=(hbm,) * 3,
            scratch_shapes=[pltpu.SemaphoreType.DMA((3,))],
            name="store",
        )(*(pltpu.with_memory_space_constraint(r, pltpu.VMEM) for r in results))
        return leaf_out, parent_out[:, None, :], root_out

    return jax.shard_map(
        shards,
        mesh=mesh,
        in_specs=(
            P(None, "leaf", "rows"),
            P(None, "leaf", "rows"),
            P(None, ("leaf", "rows")),
            P("leaf", "rows", None),
            P("leaf", "rows", None),
            P("leaf", "rows"),
            P("leaf"),
            P("leaf", "rows", None),
            P("leaf", "rows", None),
            P("leaf", "rows"),
            P("leaf"),
            P("rows", None),
        ),
        out_specs=(P(None, "leaf", "rows"), P(None, "leaf", "rows"), P(None, ("leaf", "rows"))),
        check_vma=False,
    )
```

```python
import functools

import jax
import jax.numpy as jnp
from jax import lax
from jax.experimental import pallas as pl
from jax.experimental.pallas import tpu as pltpu
from jax.sharding import PartitionSpec as P

F32 = jnp.float32
BF16 = jnp.bfloat16
LANES = 128
HALF = 64
WIDE = 256
NT = (((1,), (1,)), ((), ()))
PHASES = 16
BULK = 15


def dot(a, b):
    return jnp.dot(a, b, preferred_element_type=F32)


def dot_nt(a, b):
    return lax.dot_general(a, b, NT, preferred_element_type=F32)


def swap_halves(x):
    return pltpu.roll(x, HALF, 1)


def kernel(
    n,
    groups,
    leaf_rhs_hbm,
    parent_rhs_hbm,
    root_rhs_hbm,
    leaf_rows_hbm,
    leaf_height_hbm,
    parent_rows_hbm,
    parent_height_hbm,
    leaf_inv_hbm,
    leaf_panel_hbm,
    parent_inv_hbm,
    parent_panel_hbm,
    root_inv_hbm,
    leaf_out,
    parent_out,
    root_out,
    leaf_rhs,
    parent_rhs,
    root_rhs,
    leaf_rows,
    leaf_height,
    parent_rows,
    parent_height,
    leaf_inv,
    leaf_panel,
    parent_inv,
    parent_panel,
    root_inv,
    panel_cols,
    all_rows,
    onehot,
    onehot_p,
    xs,
    panel_root,
    terms,
    g1,
    g2,
    s3p,
    r3p,
    s3r,
    r3r,
    g4,
    s6,
    r6,
    g7a,
    g7b,
    s8,
    r8,
    g9,
    s11,
    r11,
    g12,
    s13,
    r13,
    s14,
    r14,
    load_sem,
    send_sem,
    recv_sem,
):
    group = lax.axis_index("leaf")
    me = lax.axis_index("rows")

    barrier = pltpu.get_barrier_semaphore()

    if n == 32:
        z, x, core = lax.div(me, 8), lax.rem(lax.div(me, 2), 4), lax.rem(me, 2)
    order = [(x, c) for x in (2, 3, 1, 0) for c in (1, 0)]

    def each_peer(act):
        if n != 32:
            lax.fori_loop(1, n, lambda i, carry: (act(lax.rem(me + i, n)), carry)[1], 0)
            return

        def ring(i, carry):
            base = 8 * lax.rem(z + (2 + i) - 4 * lax.div(i, 2) + lax.div(i, 2), 4)
            for dx, dc in order:
                act(base + 2 * lax.rem(x + dx, 4) + lax.rem(core + dc, 2))
            return carry

        lax.fori_loop(0, 3, ring, 0)
        for dx, dc in order[:-1]:
            act(8 * z + 2 * lax.rem(x + dx, 4) + lax.rem(core + dc, 2))

    each_peer(lambda peer: pl.semaphore_signal(barrier, inc=1, device_id={"rows": peer}))
    for i in range(1, groups):
        pl.semaphore_signal(barrier, inc=1, device_id={"leaf": lax.rem(group + i, groups)})

    own_cols = parent_panel_hbm.at[:, pl.ds(pl.multiple_of(me * LANES, LANES), LANES)]
    loads = [
        pltpu.make_async_copy(src, dst, load_sem.at[i])
        for i, (src, dst) in enumerate(
            (
                (leaf_rhs_hbm, leaf_rhs),
                (leaf_rows_hbm, leaf_rows),
                (leaf_height_hbm, leaf_height),
                (parent_rows_hbm, parent_rows),
                (parent_height_hbm, parent_height),
                (root_rhs_hbm, root_rhs),
                (parent_rhs_hbm, parent_rhs),
                (leaf_inv_hbm, leaf_inv),
                (leaf_panel_hbm, leaf_panel),
                (parent_inv_hbm, parent_inv),
                (root_inv_hbm, root_inv),
                (own_cols, panel_cols.at[me]),
            )
        )
    ]
    for copy in loads:
        copy.start()

    def load_cols(c, carry):
        cols = pl.ds(pl.multiple_of(c * LANES, LANES), LANES)
        pltpu.make_async_copy(
            parent_panel_hbm.at[:, cols], parent_panel.at[c], load_sem.at[12]
        ).start()
        return carry

    lax.fori_loop(0, n, load_cols, 0)

    low = lax.broadcasted_iota(jnp.int32, (8, LANES), 1) < HALF
    low16 = lax.broadcasted_iota(jnp.int32, (16, LANES), 1) < HALF

    def drain(ref, sem, count):
        view = ref.at[pl.ds(0, count)]
        pltpu.make_async_copy(view, view, sem).wait()

    def gather_start(ref, value, phase):
        ref[me] = value
        each_peer(
            lambda peer: pltpu.make_async_remote_copy(
                src_ref=ref.at[me],
                dst_ref=ref.at[me],
                send_sem=send_sem.at[phase],
                recv_sem=recv_sem.at[phase],
                device_id={"rows": peer},
            ).start()
        )

    def gather_wait(ref, phase):
        drain(ref, recv_sem.at[phase], n - 1)

    def scatter_start(src, dst, phase):
        each_peer(
            lambda peer: pltpu.make_async_remote_copy(
                src_ref=src.at[peer],
                dst_ref=dst.at[me],
                send_sem=send_sem.at[phase],
                recv_sem=recv_sem.at[phase],
                device_id={"rows": peer},
            ).start()
        )
        dst[me] = src[me]

    def send_panel(turn):
        def send(i, carry):
            if n == 32:
                dz, dc = lax.div(i, 2), lax.rem(i, 2)
                dx = lax.rem(turn + 4 - dz, 4)
                row = 8 * lax.rem(z + dz, 4) + 2 * lax.rem(x + dx, 4)
                peer = row + lax.rem(core + dc, 2)
            else:
                peer = lax.rem(me + turn * n // 4 + i, n)
            pltpu.make_async_remote_copy(
                src_ref=parent_panel.at[peer],
                dst_ref=panel_cols.at[me],
                send_sem=send_sem.at[BULK],
                recv_sem=recv_sem.at[BULK],
                device_id={"rows": peer},
            ).start()
            return carry

        lax.fori_loop(0 if turn else 1, n // 4, send, 0)

    def scatter_sum(dst, phase):
        drain(dst, recv_sem.at[phase], n - 1)
        return jnp.sum(dst[...].astype(F32), axis=0)

    def pack_rhs():
        tops = [
            jnp.concatenate([leaf_rhs[:, 2 * a, :], leaf_rhs[:, 2 * a + 1, :]], axis=1)
            for a in range(2)
        ]
        return jnp.concatenate(tops, axis=0).astype(BF16)

    def unpack(ref):
        for c in range(n // 2):
            even = ref[2 * c].astype(F32)
            odd = ref[2 * c + 1].astype(F32)
            cols = pl.ds(c * LANES, LANES)
            xs[0:16, cols] = jnp.where(low16, even, swap_halves(odd)).astype(BF16)
            xs[16:32, cols] = jnp.where(low16, swap_halves(even), odd).astype(BF16)

    def pack_terms(dst):
        for c in range(n // 2):
            cols = pl.ds(c * LANES, LANES)
            first, second = [], []
            for a in range(2):
                even = terms[pl.ds(16 * a, 8), cols]
                odd = terms[pl.ds(16 * a + 8, 8), cols]
                first.append(jnp.where(low, even, swap_halves(odd)))
                second.append(jnp.where(low, swap_halves(even), odd))
            dst[2 * c] = jnp.concatenate(first, axis=0).astype(BF16)
            dst[2 * c + 1] = jnp.concatenate(second, axis=0).astype(BF16)

    def columns(ref):
        return jnp.concatenate([ref[c] for c in range(n)], axis=1)

    blocks = n // 2

    def spread(value, where_at, first):
        pair = jnp.concatenate([value, value], axis=0).astype(BF16)
        second = lax.broadcasted_iota(jnp.int32, pair.shape, 0) >= 8
        at = jnp.concatenate([where_at, where_at], axis=0) - jnp.where(second, 1, 0)
        at = at.astype(F32).astype(BF16)
        return jnp.concatenate(
            [
                jnp.where(at == jnp.array(first + q, BF16), pair, jnp.array(0.0, BF16))
                for q in range(0, blocks, 2)
            ],
            axis=0,
        )

    def put_blocks(dst, acc):
        for c in range(n):
            part = acc[8 * (c // 2) : 8 * (c // 2) + 8, LANES * (c % 2) : LANES * (c % 2 + 1)]
            dst[c] = part.astype(dst.dtype)

    def get_blocks(ref):
        return jnp.concatenate(
            [jnp.concatenate([ref[2 * q], ref[2 * q + 1]], axis=1) for q in range(blocks)], axis=0
        )

    def pick(table, where_at, first):
        total = jnp.zeros(where_at.shape, F32)
        for q in range(blocks):
            total += jnp.where(where_at == first + q, table[8 * q : 8 * q + 8, :], 0.0)
        return total

    def root_order(first, last):
        at = jnp.broadcast_to(parent_at[0:1, :], (16, n * LANES)).astype(F32).astype(BF16)
        for q in range(first, last):
            mine = at == jnp.array(q, BF16)
            chosen = jnp.concatenate(
                [
                    jnp.where(mine, onehot_p[16 * i : 16 * i + 16, :], jnp.array(0.0, BF16))
                    for i in range(WIDE // 16)
                ],
                axis=0,
            )
            panel_root[pl.ds(q * WIDE, WIDE), :] = dot(chosen, cols_of).astype(BF16)

    loads[0].wait()
    packed_rhs = pack_rhs()
    pl.semaphore_wait(barrier, n - 1 + groups - 1)
    gather_start(g1, packed_rhs, 0)
    for copy in loads[1:7]:
        copy.wait()
    all_rows[me] = parent_rows[...]
    each_peer(
        lambda peer: pltpu.make_async_remote_copy(
            src_ref=all_rows.at[me],
            dst_ref=all_rows.at[me],
            send_sem=send_sem.at[4],
            recv_sem=recv_sem.at[4],
            device_id={"rows": peer},
        ).start()
    )
    pltpu.make_async_copy(parent_panel, parent_panel, load_sem.at[12]).wait()
    send_panel(2)

    piece = leaf_rows.shape[1]
    at_list, low_list = [], []
    for s in range(4):
        rows_s = leaf_rows[s : s + 1, :]
        pos = me * piece + lax.broadcasted_iota(jnp.int32, (1, piece), 1)
        at_list.append(jnp.where(pos < leaf_height[s], rows_s >> 8, -1))
        low_list.append(rows_s & (WIDE - 1))
    height = 4 * piece
    leaf_at = jnp.broadcast_to(jnp.concatenate(at_list, axis=1), (8, height))
    leaf_low = jnp.concatenate(low_list, axis=1)
    onehot[...] = jnp.where(
        lax.broadcasted_iota(jnp.int32, (WIDE, height), 0) == leaf_low, 1.0, 0.0
    ).astype(BF16)

    loads[7].wait()
    gather_wait(g1, 0)
    unpack(g1)
    full = dot_nt(xs[...], leaf_inv[...])
    ly = jnp.concatenate(
        [
            jnp.where(low, full[0:8, 0:LANES], full[16:24, 0:LANES]),
            jnp.where(low, full[8:16, LANES:], full[24:32, LANES:]),
        ],
        axis=0,
    )
    gather_start(g2, ly.astype(BF16), 1)
    send_panel(1)

    drain(all_rows, recv_sem.at[4], n - 1)
    rows_p = jnp.concatenate([all_rows[c] for c in range(n)], axis=1)
    pos_p = lax.broadcasted_iota(jnp.int32, rows_p.shape, 1)
    parent_at = jnp.broadcast_to(
        jnp.where(pos_p < parent_height[0], rows_p >> 8, -1), (8, n * LANES)
    )
    onehot_p[...] = jnp.where(
        lax.broadcasted_iota(jnp.int32, onehot_p.shape, 0) == (rows_p & (WIDE - 1)), 1.0, 0.0
    ).astype(BF16)

    loads[8].wait()
    gather_wait(g2, 1)
    unpack(g2)
    updates = []
    acc = jnp.zeros((8 * blocks, WIDE), F32)
    for s in range(4):
        a, b = s // 2, s % 2
        cols = slice(s * piece, (s + 1) * piece)
        got = dot_nt(xs[16 * b : 16 * b + 16, :], leaf_panel[cols, :])
        updates.append(got[8 * a : 8 * a + 8, :])
        acc += dot_nt(spread(updates[s], leaf_at[:, cols], 0), onehot[:, cols])
    put_blocks(s3p, acc)
    scatter_start(s3p, r3p, 2)
    send_panel(3)
    acc = jnp.zeros((8 * blocks, WIDE), F32)
    for s in range(4):
        cols = slice(s * piece, (s + 1) * piece)
        acc += dot_nt(spread(updates[s], leaf_at[:, cols], blocks), onehot[:, cols])
    put_blocks(s3r, acc)
    pacc = scatter_sum(r3p, 2)

    prb = (parent_rhs[...] - pacc).astype(BF16)
    gather_start(g4, prb, 3)
    scatter_start(s3r, r3r, 10)
    send_panel(0)
    loads[9].wait()
    loads[11].wait()
    gather_wait(g4, 3)
    py = dot_nt(columns(g4), parent_inv[...])
    drain(panel_cols, recv_sem.at[BULK], n - 1)
    cols_of = panel_cols[...].reshape(n * LANES, LANES)
    pyb = py.astype(BF16)
    acc = jnp.zeros((8 * blocks, WIDE), F32)
    chunk = 4 * LANES
    for c in range(0, n * LANES, chunk):
        cols = slice(c, c + chunk)
        got = dot_nt(pyb, cols_of[cols, :])
        acc += dot_nt(spread(got, parent_at[:, cols], 0), onehot_p[:, cols])
    put_blocks(s6, acc)
    width = root_rhs.shape[1]
    per_slab = LANES // width
    slab = lax.div(group * n + me, per_slab)
    part = lax.rem(me, per_slab)
    lane_part = lax.broadcasted_iota(jnp.int32, (8, LANES), 1) // width
    mine = jnp.concatenate([root_rhs[...]] * per_slab, axis=1)
    s6[slab] = (s6[slab].astype(F32) - jnp.where(lane_part == part, mine, 0.0)).astype(BF16)
    scatter_start(s6, r6, 5)
    root_order(0, (2 * blocks) // 8)
    racc = scatter_sum(r3r, 10)
    partial = scatter_sum(r6, 5) + racc

    g7a[group] = partial
    for i in range(1, groups):
        pltpu.make_async_remote_copy(
            src_ref=g7a.at[group],
            dst_ref=g7a.at[group],
            send_sem=send_sem.at[6],
            recv_sem=recv_sem.at[6],
            device_id={"leaf": lax.rem(group + i, groups)},
        ).start()
    root_order((2 * blocks) // 8, (3 * blocks) // 8)
    drain(g7a, recv_sem.at[6], groups - 1)
    rrb = (-jnp.sum(g7a[...], axis=0)).astype(BF16)
    gather_start(g7b, rrb, 7)
    root_order((3 * blocks) // 8, (5 * blocks) // 8)
    loads[10].wait()
    gather_wait(g7b, 7)
    ry = dot_nt(columns(g7b), root_inv[...])
    root_term = dot(ry.astype(BF16), root_inv[...])
    for c in range(n):
        s8[c] = root_term[:, c * LANES : (c + 1) * LANES].astype(BF16)
    scatter_start(s8, r8, 8)
    root_order((5 * blocks) // 8, (7 * blocks) // 8)
    root_slab = scatter_sum(r8, 8)
    gather_start(g9, root_slab.astype(BF16), 9)
    root_order((7 * blocks) // 8, blocks)
    gather_wait(g9, 9)

    pt = dot(columns(g9), panel_root[...])
    pvb = (py - pt).astype(BF16)
    parent_term = dot(pvb, parent_inv[...])
    for c in range(n):
        s11[c] = parent_term[:, c * LANES : (c + 1) * LANES].astype(BF16)
    scatter_start(s11, r11, 11)
    rxb = get_blocks(g9)
    root_anc = [
        pick(
            dot(rxb, onehot[:, s * piece : (s + 1) * piece]),
            leaf_at[:, s * piece : (s + 1) * piece],
            blocks,
        )
        for s in range(4)
    ]
    mine = jnp.where(lane_part == part, g9[slab].astype(F32), 0.0)
    root_out[...] = functools.reduce(
        lambda x, y: x + y, [mine[:, k * width : (k + 1) * width] for k in range(per_slab)]
    )
    parent_sol = scatter_sum(r11, 11)
    gather_start(g12, parent_sol.astype(BF16), 12)
    parent_out[...] = parent_sol
    gather_wait(g12, 12)

    pxb = get_blocks(g12)
    for s in range(4):
        cols = slice(s * piece, (s + 1) * piece)
        got = (root_anc[s] + pick(dot(pxb, onehot[:, cols]), leaf_at[:, cols], 0)).astype(BF16)
        terms[pl.ds(8 * s, 8), :] = dot(got, leaf_panel[pl.ds(s * piece, piece), :])
    pack_terms(s13)
    scatter_start(s13, r13, 13)
    lvb = ly - scatter_sum(r13, 13)
    none = jnp.zeros((8, LANES), F32)
    rows_of = []
    for s in range(4):
        a, b = s // 2, s % 2
        held = jnp.where(low if b == 0 else ~low, lvb[8 * a : 8 * a + 8, :], 0.0)
        rows_of.append(jnp.concatenate([held, none] if a == 0 else [none, held], axis=1))
    terms[...] = dot(jnp.concatenate(rows_of, axis=0).astype(BF16), leaf_inv[...])
    pack_terms(s14)
    scatter_start(s14, r14, 14)
    result = scatter_sum(r14, 14)
    for a in range(2):
        rows = result[8 * a : 8 * a + 8, :]
        leaf_out[:, 2 * a, :] = rows[:, :HALF]
        leaf_out[:, 2 * a + 1, :] = swap_halves(rows)[:, :HALF]

    for phase, ref in enumerate(
        (g1, g2, r3p, g4, all_rows, r6, g7a, g7b, r8, g9, r3r, r11, g12, r13, r14, panel_cols)
    ):
        drain(ref, send_sem.at[phase], (groups if phase == 6 else n) - 1)


def store(count, *refs):
    copies = [
        pltpu.make_async_copy(refs[i], refs[count + i], refs[-1].at[i]) for i in range(count)
    ]
    for copy in copies:
        copy.start()
    for copy in copies:
        copy.wait()


def solution(mesh):
    n = mesh.shape["rows"]
    groups = mesh.shape["leaf"]

    def shards(
        leaf_rhs,
        parent_rhs,
        root_rhs,
        leaf_inv,
        leaf_panel,
        leaf_rows,
        leaf_height,
        parent_inv,
        parent_panel,
        parent_rows,
        parent_height,
        root_inv,
    ):
        leaf_cols = leaf_inv.shape[2]
        cols = root_inv.shape[1]
        height = 4 * leaf_panel.shape[1]
        packed = (16, LANES)
        vmem = pl.BlockSpec(memory_space=pltpu.VMEM)
        hbm = pl.BlockSpec(memory_space=pltpu.HBM)
        slabs = (n, 8, LANES)
        buffers = [
            ((n, *packed), BF16),
            ((n, *packed), BF16),
            (slabs, BF16),
            (slabs, BF16),
            (slabs, BF16),
            (slabs, BF16),
            (slabs, BF16),
            (slabs, BF16),
            (slabs, BF16),
            ((groups, 8, LANES), F32),
            (slabs, BF16),
            (slabs, BF16),
            (slabs, BF16),
            (slabs, BF16),
            (slabs, BF16),
            (slabs, BF16),
            (slabs, BF16),
            ((n, *packed), BF16),
            ((n, *packed), BF16),
            ((n, *packed), BF16),
            ((n, *packed), BF16),
        ]
        leaf_out, parent_out, root_out = pl.pallas_call(
            functools.partial(kernel, n, groups),
            out_shape=(
                jax.ShapeDtypeStruct((8, 4, HALF), F32),
                jax.ShapeDtypeStruct((8, LANES), F32),
                jax.ShapeDtypeStruct(root_rhs.shape, F32),
            ),
            in_specs=[hbm] * 12,
            out_specs=(vmem, vmem, vmem),
            scratch_shapes=[
                pltpu.VMEM(leaf_rhs.shape, F32),
                pltpu.VMEM((8, LANES), F32),
                pltpu.VMEM(root_rhs.shape, F32),
                pltpu.VMEM(leaf_rows.shape, jnp.int32),
                pltpu.SMEM(leaf_height.shape, jnp.int32),
                pltpu.VMEM(parent_rows.shape, jnp.int32),
                pltpu.SMEM(parent_height.shape, jnp.int32),
                pltpu.VMEM((256, leaf_cols), BF16),
                pltpu.VMEM((height, leaf_cols), BF16),
                pltpu.VMEM((LANES, cols), BF16),
                pltpu.VMEM((n, LANES, LANES), BF16),
                pltpu.VMEM((LANES, cols), BF16),
                pltpu.VMEM((n, LANES, LANES), BF16),
                pltpu.VMEM((n, 1, LANES), jnp.int32),
                pltpu.VMEM((WIDE, height), BF16),
                pltpu.VMEM((WIDE, cols), BF16),
                pltpu.VMEM((32, leaf_cols), BF16),
                pltpu.VMEM((cols, LANES), BF16),
                pltpu.VMEM((32, leaf_cols), F32),
            ]
            + [pltpu.VMEM(shape, kind) for shape, kind in buffers]
            + [
                pltpu.SemaphoreType.DMA((13,)),
                pltpu.SemaphoreType.DMA((PHASES,)),
                pltpu.SemaphoreType.DMA((PHASES,)),
            ],
            compiler_params=pltpu.CompilerParams(
                collective_id=0, has_side_effects=True, vmem_limit_bytes=48 << 20
            ),
            name="solve",
        )(
            *(
                x if x.size == 1 else pltpu.with_memory_space_constraint(x, pltpu.HBM)
                for x in (
                    leaf_rhs,
                    parent_rhs[:, 0, :],
                    root_rhs,
                    leaf_rows,
                    leaf_height,
                    parent_rows,
                    parent_height,
                    leaf_inv.reshape(-1, leaf_cols),
                    leaf_panel.reshape(-1, leaf_cols),
                    parent_inv[0],
                    parent_panel[0],
                    root_inv,
                )
            )
        )
        results = (leaf_out, parent_out, root_out)
        leaf_out, parent_out, root_out = pl.pallas_call(
            functools.partial(store, 3),
            out_shape=tuple(jax.ShapeDtypeStruct(r.shape, r.dtype) for r in results),
            in_specs=[vmem] * 3,
            out_specs=(hbm,) * 3,
            scratch_shapes=[pltpu.SemaphoreType.DMA((3,))],
            name="store",
        )(*(pltpu.with_memory_space_constraint(r, pltpu.VMEM) for r in results))
        return leaf_out, parent_out[:, None, :], root_out

    return jax.shard_map(
        shards,
        mesh=mesh,
        in_specs=(
            P(None, "leaf", "rows"),
            P(None, "leaf", "rows"),
            P(None, ("leaf", "rows")),
            P("leaf", "rows", None),
            P("leaf", "rows", None),
            P("leaf", "rows"),
            P("leaf"),
            P("leaf", "rows", None),
            P("leaf", "rows", None),
            P("leaf", "rows"),
            P("leaf"),
            P("rows", None),
        ),
        out_specs=(P(None, "leaf", "rows"), P(None, "leaf", "rows"), P(None, ("leaf", "rows"))),
        check_vma=False,
    )
```

```python
import functools

import jax
import jax.numpy as jnp
from jax import lax
from jax.experimental import pallas as pl
from jax.experimental.pallas import tpu as pltpu
from jax.sharding import PartitionSpec as P

F32 = jnp.float32
BF16 = jnp.bfloat16
LANES = 128
HALF = 64
WIDE = 256
NT = (((1,), (1,)), ((), ()))
PHASES = 16
BULK = 15


def dot(a, b):
    return jnp.dot(a, b, preferred_element_type=F32)


def dot_nt(a, b):
    return lax.dot_general(a, b, NT, preferred_element_type=F32)


def swap_halves(x):
    return pltpu.roll(x, HALF, 1)


def kernel(
    n,
    groups,
    leaf_rhs_hbm,
    parent_rhs_hbm,
    root_rhs_hbm,
    leaf_rows_hbm,
    leaf_height_hbm,
    parent_rows_hbm,
    parent_height_hbm,
    leaf_inv_hbm,
    leaf_panel_hbm,
    parent_inv_hbm,
    parent_panel_hbm,
    root_inv_hbm,
    leaf_out,
    parent_out,
    root_out,
    leaf_rhs,
    parent_rhs,
    root_rhs,
    leaf_rows,
    leaf_height,
    parent_rows,
    parent_height,
    leaf_inv,
    leaf_panel,
    parent_inv,
    parent_panel,
    root_inv,
    panel_cols,
    all_rows,
    onehot,
    onehot_p,
    xs,
    panel_root,
    terms,
    g1,
    g2,
    s3p,
    r3p,
    s3r,
    r3r,
    g4,
    s6,
    r6,
    g7a,
    g7b,
    s8,
    r8,
    g9,
    s11,
    r11,
    g12,
    s13,
    r13,
    s14,
    r14,
    load_sem,
    send_sem,
    recv_sem,
):
    group = lax.axis_index("leaf")
    me = lax.axis_index("rows")

    barrier = pltpu.get_barrier_semaphore()

    if n == 32:
        z, x, core = lax.div(me, 8), lax.rem(lax.div(me, 2), 4), lax.rem(me, 2)
    order = [(x, c) for x in (2, 3, 1, 0) for c in (1, 0)]

    def each_peer(act):
        if n != 32:
            lax.fori_loop(1, n, lambda i, carry: (act(lax.rem(me + i, n)), carry)[1], 0)
            return

        def ring(i, carry):
            base = 8 * lax.rem(z + (2 + i) - 4 * lax.div(i, 2) + lax.div(i, 2), 4)
            for dx, dc in order:
                act(base + 2 * lax.rem(x + dx, 4) + lax.rem(core + dc, 2))
            return carry

        lax.fori_loop(0, 3, ring, 0)
        for dx, dc in order[:-1]:
            act(8 * z + 2 * lax.rem(x + dx, 4) + lax.rem(core + dc, 2))

    each_peer(lambda peer: pl.semaphore_signal(barrier, inc=1, device_id={"rows": peer}))
    for i in range(1, groups):
        pl.semaphore_signal(barrier, inc=1, device_id={"leaf": lax.rem(group + i, groups)})

    own_cols = parent_panel_hbm.at[:, pl.ds(pl.multiple_of(me * LANES, LANES), LANES)]
    loads = [
        pltpu.make_async_copy(src, dst, load_sem.at[i])
        for i, (src, dst) in enumerate(
            (
                (leaf_rhs_hbm, leaf_rhs),
                (leaf_rows_hbm, leaf_rows),
                (leaf_height_hbm, leaf_height),
                (parent_rows_hbm, parent_rows),
                (parent_height_hbm, parent_height),
                (root_rhs_hbm, root_rhs),
                (parent_rhs_hbm, parent_rhs),
                (leaf_inv_hbm, leaf_inv),
                (leaf_panel_hbm, leaf_panel),
                (parent_inv_hbm, parent_inv),
                (root_inv_hbm, root_inv),
                (own_cols, panel_cols.at[me]),
            )
        )
    ]
    for copy in loads:
        copy.start()

    def load_cols(c, carry):
        cols = pl.ds(pl.multiple_of(c * LANES, LANES), LANES)
        pltpu.make_async_copy(
            parent_panel_hbm.at[:, cols], parent_panel.at[c], load_sem.at[12]
        ).start()
        return carry

    lax.fori_loop(0, n, load_cols, 0)

    low = lax.broadcasted_iota(jnp.int32, (8, LANES), 1) < HALF
    low16 = lax.broadcasted_iota(jnp.int32, (16, LANES), 1) < HALF

    def drain(ref, sem, count):
        view = ref.at[pl.ds(0, count)]
        pltpu.make_async_copy(view, view, sem).wait()

    def gather_start(ref, value, phase):
        ref[me] = value
        each_peer(
            lambda peer: pltpu.make_async_remote_copy(
                src_ref=ref.at[me],
                dst_ref=ref.at[me],
                send_sem=send_sem.at[phase],
                recv_sem=recv_sem.at[phase],
                device_id={"rows": peer},
            ).start()
        )

    def gather_wait(ref, phase):
        drain(ref, recv_sem.at[phase], n - 1)

    def scatter_start(src, dst, phase):
        each_peer(
            lambda peer: pltpu.make_async_remote_copy(
                src_ref=src.at[peer],
                dst_ref=dst.at[me],
                send_sem=send_sem.at[phase],
                recv_sem=recv_sem.at[phase],
                device_id={"rows": peer},
            ).start()
        )
        dst[me] = src[me]

    def send_panel(turn):
        if n == 32:
            extra = {2: (2, 2), 1: (1, 3), 3: (3, 1)}[turn]
            steps = [(dz, (turn - dz) % 4) for dz in range(4)] + [extra]
            moves = [(dz, dx, dc) for dz, dx in steps for dc in range(2)]
            peers = [
                8 * lax.rem(z + dz, 4) + 2 * lax.rem(x + dx, 4) + lax.rem(core + dc, 2)
                for dz, dx, dc in moves + ([(0, 0, 1)] if turn == 2 else [])
            ]
        else:
            peers = [lax.rem(me + i, n) for i in range(turn, n, 3)]
        for peer in peers:
            pltpu.make_async_remote_copy(
                src_ref=parent_panel.at[peer],
                dst_ref=panel_cols.at[me],
                send_sem=send_sem.at[BULK],
                recv_sem=recv_sem.at[BULK],
                device_id={"rows": peer},
            ).start()

    def scatter_sum(dst, phase):
        drain(dst, recv_sem.at[phase], n - 1)
        return jnp.sum(dst[...].astype(F32), axis=0)

    def pack_rhs():
        tops = [
            jnp.concatenate([leaf_rhs[:, 2 * a, :], leaf_rhs[:, 2 * a + 1, :]], axis=1)
            for a in range(2)
        ]
        return jnp.concatenate(tops, axis=0).astype(BF16)

    def unpack(ref):
        for c in range(n // 2):
            even = ref[2 * c].astype(F32)
            odd = ref[2 * c + 1].astype(F32)
            cols = pl.ds(c * LANES, LANES)
            xs[0:16, cols] = jnp.where(low16, even, swap_halves(odd)).astype(BF16)
            xs[16:32, cols] = jnp.where(low16, swap_halves(even), odd).astype(BF16)

    def pack_terms(dst):
        for c in range(n // 2):
            cols = pl.ds(c * LANES, LANES)
            first, second = [], []
            for a in range(2):
                even = terms[pl.ds(16 * a, 8), cols]
                odd = terms[pl.ds(16 * a + 8, 8), cols]
                first.append(jnp.where(low, even, swap_halves(odd)))
                second.append(jnp.where(low, swap_halves(even), odd))
            dst[2 * c] = jnp.concatenate(first, axis=0).astype(BF16)
            dst[2 * c + 1] = jnp.concatenate(second, axis=0).astype(BF16)

    def columns(ref):
        return jnp.concatenate([ref[c] for c in range(n)], axis=1)

    blocks = n // 2

    def spread(value, where_at, first):
        pair = jnp.concatenate([value, value], axis=0).astype(BF16)
        second = lax.broadcasted_iota(jnp.int32, pair.shape, 0) >= 8
        at = jnp.concatenate([where_at, where_at], axis=0) - jnp.where(second, 1, 0)
        at = at.astype(F32).astype(BF16)
        return jnp.concatenate(
            [
                jnp.where(at == jnp.array(first + q, BF16), pair, jnp.array(0.0, BF16))
                for q in range(0, blocks, 2)
            ],
            axis=0,
        )

    def put_blocks(dst, acc):
        for c in range(n):
            part = acc[8 * (c // 2) : 8 * (c // 2) + 8, LANES * (c % 2) : LANES * (c % 2 + 1)]
            dst[c] = part.astype(dst.dtype)

    def get_blocks(ref):
        return jnp.concatenate(
            [jnp.concatenate([ref[2 * q], ref[2 * q + 1]], axis=1) for q in range(blocks)], axis=0
        )

    def pick(table, where_at, first):
        total = jnp.zeros(where_at.shape, F32)
        for q in range(blocks):
            total += jnp.where(where_at == first + q, table[8 * q : 8 * q + 8, :], 0.0)
        return total

    def root_order(first, last):
        at = jnp.broadcast_to(parent_at[0:1, :], (16, n * LANES)).astype(F32).astype(BF16)
        for q in range(first, last):
            mine = at == jnp.array(q, BF16)
            chosen = jnp.concatenate(
                [
                    jnp.where(mine, onehot_p[16 * i : 16 * i + 16, :], jnp.array(0.0, BF16))
                    for i in range(WIDE // 16)
                ],
                axis=0,
            )
            panel_root[pl.ds(q * WIDE, WIDE), :] = dot(chosen, cols_of).astype(BF16)

    loads[0].wait()
    packed_rhs = pack_rhs()
    pl.semaphore_wait(barrier, n - 1 + groups - 1)
    gather_start(g1, packed_rhs, 0)
    for copy in loads[1:7]:
        copy.wait()
    all_rows[me] = parent_rows[...]
    each_peer(
        lambda peer: pltpu.make_async_remote_copy(
            src_ref=all_rows.at[me],
            dst_ref=all_rows.at[me],
            send_sem=send_sem.at[4],
            recv_sem=recv_sem.at[4],
            device_id={"rows": peer},
        ).start()
    )
    pltpu.make_async_copy(parent_panel, parent_panel, load_sem.at[12]).wait()
    send_panel(2)

    piece = leaf_rows.shape[1]
    at_list, low_list = [], []
    for s in range(4):
        rows_s = leaf_rows[s : s + 1, :]
        pos = me * piece + lax.broadcasted_iota(jnp.int32, (1, piece), 1)
        at_list.append(jnp.where(pos < leaf_height[s], rows_s >> 8, -1))
        low_list.append(rows_s & (WIDE - 1))
    height = 4 * piece
    leaf_at = jnp.broadcast_to(jnp.concatenate(at_list, axis=1), (8, height))
    leaf_low = jnp.concatenate(low_list, axis=1)
    onehot[...] = jnp.where(
        lax.broadcasted_iota(jnp.int32, (WIDE, height), 0) == leaf_low, 1.0, 0.0
    ).astype(BF16)

    loads[7].wait()
    gather_wait(g1, 0)
    unpack(g1)
    full = dot_nt(xs[...], leaf_inv[...])
    ly = jnp.concatenate(
        [
            jnp.where(low, full[0:8, 0:LANES], full[16:24, 0:LANES]),
            jnp.where(low, full[8:16, LANES:], full[24:32, LANES:]),
        ],
        axis=0,
    )
    gather_start(g2, ly.astype(BF16), 1)
    send_panel(1)

    drain(all_rows, recv_sem.at[4], n - 1)
    rows_p = jnp.concatenate([all_rows[c] for c in range(n)], axis=1)
    pos_p = lax.broadcasted_iota(jnp.int32, rows_p.shape, 1)
    parent_at = jnp.broadcast_to(
        jnp.where(pos_p < parent_height[0], rows_p >> 8, -1), (8, n * LANES)
    )
    onehot_p[...] = jnp.where(
        lax.broadcasted_iota(jnp.int32, onehot_p.shape, 0) == (rows_p & (WIDE - 1)), 1.0, 0.0
    ).astype(BF16)

    loads[8].wait()
    gather_wait(g2, 1)
    unpack(g2)
    updates = []
    acc = jnp.zeros((8 * blocks, WIDE), F32)
    for s in range(4):
        a, b = s // 2, s % 2
        cols = slice(s * piece, (s + 1) * piece)
        got = dot_nt(xs[16 * b : 16 * b + 16, :], leaf_panel[cols, :])
        updates.append(got[8 * a : 8 * a + 8, :])
        acc += dot_nt(spread(updates[s], leaf_at[:, cols], 0), onehot[:, cols])
    put_blocks(s3p, acc)
    scatter_start(s3p, r3p, 2)
    send_panel(3)
    acc = jnp.zeros((8 * blocks, WIDE), F32)
    for s in range(4):
        cols = slice(s * piece, (s + 1) * piece)
        acc += dot_nt(spread(updates[s], leaf_at[:, cols], blocks), onehot[:, cols])
    put_blocks(s3r, acc)
    pacc = scatter_sum(r3p, 2)

    prb = (parent_rhs[...] - pacc).astype(BF16)
    gather_start(g4, prb, 3)
    scatter_start(s3r, r3r, 10)
    loads[9].wait()
    loads[11].wait()
    gather_wait(g4, 3)
    py = dot_nt(columns(g4), parent_inv[...])
    drain(panel_cols, recv_sem.at[BULK], n - 1)
    cols_of = panel_cols[...].reshape(n * LANES, LANES)
    pyb = py.astype(BF16)
    acc = jnp.zeros((8 * blocks, WIDE), F32)
    chunk = 4 * LANES
    for c in range(0, n * LANES, chunk):
        cols = slice(c, c + chunk)
        got = dot_nt(pyb, cols_of[cols, :])
        acc += dot_nt(spread(got, parent_at[:, cols], 0), onehot_p[:, cols])
    put_blocks(s6, acc)
    width = root_rhs.shape[1]
    per_slab = LANES // width
    slab = lax.div(group * n + me, per_slab)
    part = lax.rem(me, per_slab)
    lane_part = lax.broadcasted_iota(jnp.int32, (8, LANES), 1) // width
    mine = jnp.concatenate([root_rhs[...]] * per_slab, axis=1)
    s6[slab] = (s6[slab].astype(F32) - jnp.where(lane_part == part, mine, 0.0)).astype(BF16)
    scatter_start(s6, r6, 5)
    root_order(0, (2 * blocks) // 8)
    racc = scatter_sum(r3r, 10)
    partial = scatter_sum(r6, 5) + racc

    g7a[group] = partial
    for i in range(1, groups):
        pltpu.make_async_remote_copy(
            src_ref=g7a.at[group],
            dst_ref=g7a.at[group],
            send_sem=send_sem.at[6],
            recv_sem=recv_sem.at[6],
            device_id={"leaf": lax.rem(group + i, groups)},
        ).start()
    root_order((2 * blocks) // 8, (3 * blocks) // 8)
    drain(g7a, recv_sem.at[6], groups - 1)
    rrb = (-jnp.sum(g7a[...], axis=0)).astype(BF16)
    gather_start(g7b, rrb, 7)
    root_order((3 * blocks) // 8, (5 * blocks) // 8)
    loads[10].wait()
    gather_wait(g7b, 7)
    ry = dot_nt(columns(g7b), root_inv[...])
    root_term = dot(ry.astype(BF16), root_inv[...])
    for c in range(n):
        s8[c] = root_term[:, c * LANES : (c + 1) * LANES].astype(BF16)
    scatter_start(s8, r8, 8)
    root_order((5 * blocks) // 8, (7 * blocks) // 8)
    root_slab = scatter_sum(r8, 8)
    gather_start(g9, root_slab.astype(BF16), 9)
    root_order((7 * blocks) // 8, blocks)
    gather_wait(g9, 9)

    pt = dot(columns(g9), panel_root[...])
    pvb = (py - pt).astype(BF16)
    parent_term = dot(pvb, parent_inv[...])
    for c in range(n):
        s11[c] = parent_term[:, c * LANES : (c + 1) * LANES].astype(BF16)
    scatter_start(s11, r11, 11)
    rxb = get_blocks(g9)
    root_anc = [
        pick(
            dot(rxb, onehot[:, s * piece : (s + 1) * piece]),
            leaf_at[:, s * piece : (s + 1) * piece],
            blocks,
        )
        for s in range(4)
    ]
    mine = jnp.where(lane_part == part, g9[slab].astype(F32), 0.0)
    root_out[...] = functools.reduce(
        lambda x, y: x + y, [mine[:, k * width : (k + 1) * width] for k in range(per_slab)]
    )
    parent_sol = scatter_sum(r11, 11)
    gather_start(g12, parent_sol.astype(BF16), 12)
    parent_out[...] = parent_sol
    gather_wait(g12, 12)

    pxb = get_blocks(g12)
    for s in range(4):
        cols = slice(s * piece, (s + 1) * piece)
        got = (root_anc[s] + pick(dot(pxb, onehot[:, cols]), leaf_at[:, cols], 0)).astype(BF16)
        terms[pl.ds(8 * s, 8), :] = dot(got, leaf_panel[pl.ds(s * piece, piece), :])
    pack_terms(s13)
    scatter_start(s13, r13, 13)
    lvb = ly - scatter_sum(r13, 13)
    none = jnp.zeros((8, LANES), F32)
    rows_of = []
    for s in range(4):
        a, b = s // 2, s % 2
        held = jnp.where(low if b == 0 else ~low, lvb[8 * a : 8 * a + 8, :], 0.0)
        rows_of.append(jnp.concatenate([held, none] if a == 0 else [none, held], axis=1))
    terms[...] = dot(jnp.concatenate(rows_of, axis=0).astype(BF16), leaf_inv[...])
    pack_terms(s14)
    scatter_start(s14, r14, 14)
    result = scatter_sum(r14, 14)
    for a in range(2):
        rows = result[8 * a : 8 * a + 8, :]
        leaf_out[:, 2 * a, :] = rows[:, :HALF]
        leaf_out[:, 2 * a + 1, :] = swap_halves(rows)[:, :HALF]

    for phase, ref in enumerate(
        (g1, g2, r3p, g4, all_rows, r6, g7a, g7b, r8, g9, r3r, r11, g12, r13, r14, panel_cols)
    ):
        drain(ref, send_sem.at[phase], (groups if phase == 6 else n) - 1)


def store(count, *refs):
    copies = [
        pltpu.make_async_copy(refs[i], refs[count + i], refs[-1].at[i]) for i in range(count)
    ]
    for copy in copies:
        copy.start()
    for copy in copies:
        copy.wait()


def solution(mesh):
    n = mesh.shape["rows"]
    groups = mesh.shape["leaf"]

    def shards(
        leaf_rhs,
        parent_rhs,
        root_rhs,
        leaf_inv,
        leaf_panel,
        leaf_rows,
        leaf_height,
        parent_inv,
        parent_panel,
        parent_rows,
        parent_height,
        root_inv,
    ):
        leaf_cols = leaf_inv.shape[2]
        cols = root_inv.shape[1]
        height = 4 * leaf_panel.shape[1]
        packed = (16, LANES)
        vmem = pl.BlockSpec(memory_space=pltpu.VMEM)
        hbm = pl.BlockSpec(memory_space=pltpu.HBM)
        slabs = (n, 8, LANES)
        buffers = [
            ((n, *packed), BF16),
            ((n, *packed), BF16),
            (slabs, BF16),
            (slabs, BF16),
            (slabs, BF16),
            (slabs, BF16),
            (slabs, BF16),
            (slabs, BF16),
            (slabs, BF16),
            ((groups, 8, LANES), F32),
            (slabs, BF16),
            (slabs, BF16),
            (slabs, BF16),
            (slabs, BF16),
            (slabs, BF16),
            (slabs, BF16),
            (slabs, BF16),
            ((n, *packed), BF16),
            ((n, *packed), BF16),
            ((n, *packed), BF16),
            ((n, *packed), BF16),
        ]
        leaf_out, parent_out, root_out = pl.pallas_call(
            functools.partial(kernel, n, groups),
            out_shape=(
                jax.ShapeDtypeStruct((8, 4, HALF), F32),
                jax.ShapeDtypeStruct((8, LANES), F32),
                jax.ShapeDtypeStruct(root_rhs.shape, F32),
            ),
            in_specs=[hbm] * 12,
            out_specs=(vmem, vmem, vmem),
            scratch_shapes=[
                pltpu.VMEM(leaf_rhs.shape, F32),
                pltpu.VMEM((8, LANES), F32),
                pltpu.VMEM(root_rhs.shape, F32),
                pltpu.VMEM(leaf_rows.shape, jnp.int32),
                pltpu.SMEM(leaf_height.shape, jnp.int32),
                pltpu.VMEM(parent_rows.shape, jnp.int32),
                pltpu.SMEM(parent_height.shape, jnp.int32),
                pltpu.VMEM((256, leaf_cols), BF16),
                pltpu.VMEM((height, leaf_cols), BF16),
                pltpu.VMEM((LANES, cols), BF16),
                pltpu.VMEM((n, LANES, LANES), BF16),
                pltpu.VMEM((LANES, cols), BF16),
                pltpu.VMEM((n, LANES, LANES), BF16),
                pltpu.VMEM((n, 1, LANES), jnp.int32),
                pltpu.VMEM((WIDE, height), BF16),
                pltpu.VMEM((WIDE, cols), BF16),
                pltpu.VMEM((32, leaf_cols), BF16),
                pltpu.VMEM((cols, LANES), BF16),
                pltpu.VMEM((32, leaf_cols), F32),
            ]
            + [pltpu.VMEM(shape, kind) for shape, kind in buffers]
            + [
                pltpu.SemaphoreType.DMA((13,)),
                pltpu.SemaphoreType.DMA((PHASES,)),
                pltpu.SemaphoreType.DMA((PHASES,)),
            ],
            compiler_params=pltpu.CompilerParams(
                collective_id=0, has_side_effects=True, vmem_limit_bytes=48 << 20
            ),
            name="solve",
        )(
            *(
                x if x.size == 1 else pltpu.with_memory_space_constraint(x, pltpu.HBM)
                for x in (
                    leaf_rhs,
                    parent_rhs[:, 0, :],
                    root_rhs,
                    leaf_rows,
                    leaf_height,
                    parent_rows,
                    parent_height,
                    leaf_inv.reshape(-1, leaf_cols),
                    leaf_panel.reshape(-1, leaf_cols),
                    parent_inv[0],
                    parent_panel[0],
                    root_inv,
                )
            )
        )
        results = (leaf_out, parent_out, root_out)
        leaf_out, parent_out, root_out = pl.pallas_call(
            functools.partial(store, 3),
            out_shape=tuple(jax.ShapeDtypeStruct(r.shape, r.dtype) for r in results),
            in_specs=[vmem] * 3,
            out_specs=(hbm,) * 3,
            scratch_shapes=[pltpu.SemaphoreType.DMA((3,))],
            name="store",
        )(*(pltpu.with_memory_space_constraint(r, pltpu.VMEM) for r in results))
        return leaf_out, parent_out[:, None, :], root_out

    return jax.shard_map(
        shards,
        mesh=mesh,
        in_specs=(
            P(None, "leaf", "rows"),
            P(None, "leaf", "rows"),
            P(None, ("leaf", "rows")),
            P("leaf", "rows", None),
            P("leaf", "rows", None),
            P("leaf", "rows"),
            P("leaf"),
            P("leaf", "rows", None),
            P("leaf", "rows", None),
            P("leaf", "rows"),
            P("leaf"),
            P("rows", None),
        ),
        out_specs=(P(None, "leaf", "rows"), P(None, "leaf", "rows"), P(None, ("leaf", "rows"))),
        check_vma=False,
    )
```

```python
import functools

import jax
import jax.numpy as jnp
from jax import lax
from jax.experimental import pallas as pl
from jax.experimental.pallas import tpu as pltpu
from jax.sharding import PartitionSpec as P

F32 = jnp.float32
BF16 = jnp.bfloat16
LANES = 128
HALF = 64
WIDE = 256
NT = (((1,), (1,)), ((), ()))
PHASES = 16
BULK = 15


def dot(a, b):
    return jnp.dot(a, b, preferred_element_type=F32)


def dot_nt(a, b):
    return lax.dot_general(a, b, NT, preferred_element_type=F32)


def swap_halves(x):
    return pltpu.roll(x, HALF, 1)


def kernel(
    n,
    groups,
    leaf_rhs_hbm,
    parent_rhs_hbm,
    root_rhs_hbm,
    leaf_rows_hbm,
    leaf_height_hbm,
    parent_rows_hbm,
    parent_height_hbm,
    leaf_inv_hbm,
    leaf_panel_hbm,
    parent_inv_hbm,
    parent_panel_hbm,
    root_inv_hbm,
    leaf_out,
    parent_out,
    root_out,
    leaf_rhs,
    parent_rhs,
    root_rhs,
    leaf_rows,
    leaf_height,
    parent_rows,
    parent_height,
    leaf_inv,
    leaf_panel,
    parent_inv,
    parent_panel,
    root_inv,
    panel_cols,
    all_rows,
    onehot,
    onehot_p,
    xs,
    panel_root,
    terms,
    g1,
    g2,
    s3p,
    r3p,
    s3r,
    r3r,
    g4,
    s6,
    r6,
    g7a,
    g7b,
    s8,
    r8,
    g9,
    s11,
    r11,
    g12,
    s13,
    r13,
    s14,
    r14,
    load_sem,
    send_sem,
    recv_sem,
):
    group = lax.axis_index("leaf")
    me = lax.axis_index("rows")

    barrier = pltpu.get_barrier_semaphore()

    if n == 32:
        z, x, core = lax.div(me, 8), lax.rem(lax.div(me, 2), 4), lax.rem(me, 2)
    order = [(x, c) for x in (2, 3, 1, 0) for c in (1, 0)]

    def each_peer(act):
        if n != 32:
            lax.fori_loop(1, n, lambda i, carry: (act(lax.rem(me + i, n)), carry)[1], 0)
            return

        def ring(i, carry):
            base = 8 * lax.rem(z + (2 + i) - 4 * lax.div(i, 2) + lax.div(i, 2), 4)
            for dx, dc in order:
                act(base + 2 * lax.rem(x + dx, 4) + lax.rem(core + dc, 2))
            return carry

        lax.fori_loop(0, 3, ring, 0)
        for dx, dc in order[:-1]:
            act(8 * z + 2 * lax.rem(x + dx, 4) + lax.rem(core + dc, 2))

    each_peer(lambda peer: pl.semaphore_signal(barrier, inc=1, device_id={"rows": peer}))
    for i in range(1, groups):
        pl.semaphore_signal(barrier, inc=1, device_id={"leaf": lax.rem(group + i, groups)})

    own_cols = parent_panel_hbm.at[:, pl.ds(pl.multiple_of(me * LANES, LANES), LANES)]
    loads = [
        pltpu.make_async_copy(src, dst, load_sem.at[i])
        for i, (src, dst) in enumerate(
            (
                (leaf_rhs_hbm, leaf_rhs),
                (leaf_rows_hbm, leaf_rows),
                (leaf_height_hbm, leaf_height),
                (parent_rows_hbm, parent_rows),
                (parent_height_hbm, parent_height),
                (root_rhs_hbm, root_rhs),
                (parent_rhs_hbm, parent_rhs),
                (leaf_inv_hbm, leaf_inv),
                (leaf_panel_hbm, leaf_panel),
                (parent_inv_hbm, parent_inv),
                (root_inv_hbm, root_inv),
                (own_cols, panel_cols.at[me]),
            )
        )
    ]
    for copy in loads:
        copy.start()

    def load_cols(c, carry):
        cols = pl.ds(pl.multiple_of(c * LANES, LANES), LANES)
        pltpu.make_async_copy(
            parent_panel_hbm.at[:, cols], parent_panel.at[c], load_sem.at[12]
        ).start()
        return carry

    lax.fori_loop(0, n, load_cols, 0)

    low = lax.broadcasted_iota(jnp.int32, (8, LANES), 1) < HALF
    low16 = lax.broadcasted_iota(jnp.int32, (16, LANES), 1) < HALF

    def drain(ref, sem, count):
        view = ref.at[pl.ds(0, count)]
        pltpu.make_async_copy(view, view, sem).wait()

    def gather_start(ref, value, phase):
        ref[me] = value
        each_peer(
            lambda peer: pltpu.make_async_remote_copy(
                src_ref=ref.at[me],
                dst_ref=ref.at[me],
                send_sem=send_sem.at[phase],
                recv_sem=recv_sem.at[phase],
                device_id={"rows": peer},
            ).start()
        )

    def gather_wait(ref, phase):
        drain(ref, recv_sem.at[phase], n - 1)

    def scatter_start(src, dst, phase):
        each_peer(
            lambda peer: pltpu.make_async_remote_copy(
                src_ref=src.at[peer],
                dst_ref=dst.at[me],
                send_sem=send_sem.at[phase],
                recv_sem=recv_sem.at[phase],
                device_id={"rows": peer},
            ).start()
        )
        dst[me] = src[me]

    def send_panel(turn):
        if n == 32:
            extra = {2: (2, 2), 1: (1, 3), 3: (3, 1)}[turn]
            steps = [(dz, (turn - dz) % 4) for dz in range(4)] + [extra]
            moves = [(dz, dx, dc) for dz, dx in steps for dc in range(2)]
            peers = [
                8 * lax.rem(z + dz, 4) + 2 * lax.rem(x + dx, 4) + lax.rem(core + dc, 2)
                for dz, dx, dc in moves + ([(0, 0, 1)] if turn == 2 else [])
            ]
        else:
            peers = [lax.rem(me + i, n) for i in range(turn, n, 3)]
        for peer in peers:
            pltpu.make_async_remote_copy(
                src_ref=parent_panel.at[peer],
                dst_ref=panel_cols.at[me],
                send_sem=send_sem.at[BULK],
                recv_sem=recv_sem.at[BULK],
                device_id={"rows": peer},
            ).start()

    def scatter_sum(dst, phase):
        drain(dst, recv_sem.at[phase], n - 1)
        return jnp.sum(dst[...].astype(F32), axis=0)

    def pack_rhs():
        tops = [
            jnp.concatenate([leaf_rhs[:, 2 * a, :], leaf_rhs[:, 2 * a + 1, :]], axis=1)
            for a in range(2)
        ]
        return jnp.concatenate(tops, axis=0).astype(BF16)

    def unpack(ref):
        for c in range(n // 2):
            even = ref[2 * c].astype(F32)
            odd = ref[2 * c + 1].astype(F32)
            cols = pl.ds(c * LANES, LANES)
            xs[0:16, cols] = jnp.where(low16, even, swap_halves(odd)).astype(BF16)
            xs[16:32, cols] = jnp.where(low16, swap_halves(even), odd).astype(BF16)

    def pack_terms(dst):
        for c in range(n // 2):
            cols = pl.ds(c * LANES, LANES)
            first, second = [], []
            for a in range(2):
                even = terms[pl.ds(16 * a, 8), cols]
                odd = terms[pl.ds(16 * a + 8, 8), cols]
                first.append(jnp.where(low, even, swap_halves(odd)))
                second.append(jnp.where(low, swap_halves(even), odd))
            dst[2 * c] = jnp.concatenate(first, axis=0).astype(BF16)
            dst[2 * c + 1] = jnp.concatenate(second, axis=0).astype(BF16)

    def columns(ref):
        return jnp.concatenate([ref[c] for c in range(n)], axis=1)

    blocks = n // 2

    def spread(value, where_at, first):
        pair = jnp.concatenate([value, value], axis=0).astype(BF16)
        second = lax.broadcasted_iota(jnp.int32, pair.shape, 0) >= 8
        at = jnp.concatenate([where_at, where_at], axis=0) - jnp.where(second, 1, 0)
        at = at.astype(F32).astype(BF16)
        return jnp.concatenate(
            [
                jnp.where(at == jnp.array(first + q, BF16), pair, jnp.array(0.0, BF16))
                for q in range(0, blocks, 2)
            ],
            axis=0,
        )

    def put_blocks(dst, acc):
        for c in range(n):
            part = acc[8 * (c // 2) : 8 * (c // 2) + 8, LANES * (c % 2) : LANES * (c % 2 + 1)]
            dst[c] = part.astype(dst.dtype)

    def put_product(dst, value, weights):
        for c in range(0, n, 4):
            term = dot(value, weights[:, c * LANES : (c + 4) * LANES])
            for k in range(4):
                dst[c + k] = term[:, k * LANES : (k + 1) * LANES].astype(BF16)

    def get_blocks(ref):
        return jnp.concatenate(
            [jnp.concatenate([ref[2 * q], ref[2 * q + 1]], axis=1) for q in range(blocks)], axis=0
        )

    def pick(table, where_at, first):
        total = jnp.zeros(where_at.shape, F32)
        for q in range(blocks):
            total += jnp.where(where_at == first + q, table[8 * q : 8 * q + 8, :], 0.0)
        return total

    def root_order(first, last):
        at = jnp.broadcast_to(parent_at[0:1, :], (16, n * LANES)).astype(F32).astype(BF16)
        for q in range(first, last):
            mine = at == jnp.array(q, BF16)
            chosen = jnp.concatenate(
                [
                    jnp.where(mine, onehot_p[16 * i : 16 * i + 16, :], jnp.array(0.0, BF16))
                    for i in range(WIDE // 16)
                ],
                axis=0,
            )
            panel_root[pl.ds(q * WIDE, WIDE), :] = dot(chosen, cols_of).astype(BF16)

    loads[0].wait()
    packed_rhs = pack_rhs()
    pl.semaphore_wait(barrier, n - 1 + groups - 1)
    gather_start(g1, packed_rhs, 0)
    for copy in loads[1:7]:
        copy.wait()
    all_rows[me] = parent_rows[...]
    each_peer(
        lambda peer: pltpu.make_async_remote_copy(
            src_ref=all_rows.at[me],
            dst_ref=all_rows.at[me],
            send_sem=send_sem.at[4],
            recv_sem=recv_sem.at[4],
            device_id={"rows": peer},
        ).start()
    )
    pltpu.make_async_copy(parent_panel, parent_panel, load_sem.at[12]).wait()
    send_panel(2)

    piece = leaf_rows.shape[1]
    at_list, low_list = [], []
    for s in range(4):
        rows_s = leaf_rows[s : s + 1, :]
        pos = me * piece + lax.broadcasted_iota(jnp.int32, (1, piece), 1)
        at_list.append(jnp.where(pos < leaf_height[s], rows_s >> 8, -1))
        low_list.append(rows_s & (WIDE - 1))
    height = 4 * piece
    leaf_at = jnp.broadcast_to(jnp.concatenate(at_list, axis=1), (8, height))
    leaf_low = jnp.concatenate(low_list, axis=1)
    onehot[...] = jnp.where(
        lax.broadcasted_iota(jnp.int32, (WIDE, height), 0) == leaf_low, 1.0, 0.0
    ).astype(BF16)

    loads[7].wait()
    gather_wait(g1, 0)
    unpack(g1)
    full = dot_nt(xs[...], leaf_inv[...])
    ly = jnp.concatenate(
        [
            jnp.where(low, full[0:8, 0:LANES], full[16:24, 0:LANES]),
            jnp.where(low, full[8:16, LANES:], full[24:32, LANES:]),
        ],
        axis=0,
    )
    gather_start(g2, ly.astype(BF16), 1)
    send_panel(1)

    drain(all_rows, recv_sem.at[4], n - 1)
    rows_p = jnp.concatenate([all_rows[c] for c in range(n)], axis=1)
    pos_p = lax.broadcasted_iota(jnp.int32, rows_p.shape, 1)
    parent_at = jnp.broadcast_to(
        jnp.where(pos_p < parent_height[0], rows_p >> 8, -1), (8, n * LANES)
    )
    onehot_p[...] = jnp.where(
        lax.broadcasted_iota(jnp.int32, onehot_p.shape, 0) == (rows_p & (WIDE - 1)), 1.0, 0.0
    ).astype(BF16)

    loads[8].wait()
    gather_wait(g2, 1)
    unpack(g2)
    updates = []
    acc = jnp.zeros((8 * blocks, WIDE), F32)
    for s in range(4):
        a, b = s // 2, s % 2
        cols = slice(s * piece, (s + 1) * piece)
        got = dot_nt(xs[16 * b : 16 * b + 16, :], leaf_panel[cols, :])
        updates.append(got[8 * a : 8 * a + 8, :])
        acc += dot_nt(spread(updates[s], leaf_at[:, cols], 0), onehot[:, cols])
    put_blocks(s3p, acc)
    scatter_start(s3p, r3p, 2)
    send_panel(3)
    acc = jnp.zeros((8 * blocks, WIDE), F32)
    for s in range(4):
        cols = slice(s * piece, (s + 1) * piece)
        acc += dot_nt(spread(updates[s], leaf_at[:, cols], blocks), onehot[:, cols])
    put_blocks(s3r, acc)
    pacc = scatter_sum(r3p, 2)

    prb = (parent_rhs[...] - pacc).astype(BF16)
    gather_start(g4, prb, 3)
    scatter_start(s3r, r3r, 10)
    loads[9].wait()
    loads[11].wait()
    gather_wait(g4, 3)
    py = dot_nt(columns(g4), parent_inv[...])
    drain(panel_cols, recv_sem.at[BULK], n - 1)
    cols_of = panel_cols[...].reshape(n * LANES, LANES)
    pyb = py.astype(BF16)
    acc = jnp.zeros((8 * blocks, WIDE), F32)
    chunk = 4 * LANES
    for c in range(0, n * LANES, chunk):
        cols = slice(c, c + chunk)
        got = dot_nt(pyb, cols_of[cols, :])
        acc += dot_nt(spread(got, parent_at[:, cols], 0), onehot_p[:, cols])
    put_blocks(s6, acc)
    width = root_rhs.shape[1]
    per_slab = LANES // width
    slab = lax.div(group * n + me, per_slab)
    part = lax.rem(me, per_slab)
    lane_part = lax.broadcasted_iota(jnp.int32, (8, LANES), 1) // width
    mine = jnp.concatenate([root_rhs[...]] * per_slab, axis=1)
    s6[slab] = (s6[slab].astype(F32) - jnp.where(lane_part == part, mine, 0.0)).astype(BF16)
    scatter_start(s6, r6, 5)
    root_order(0, (2 * blocks) // 8)
    racc = scatter_sum(r3r, 10)
    partial = scatter_sum(r6, 5) + racc

    g7a[group] = partial
    for i in range(1, groups):
        pltpu.make_async_remote_copy(
            src_ref=g7a.at[group],
            dst_ref=g7a.at[group],
            send_sem=send_sem.at[6],
            recv_sem=recv_sem.at[6],
            device_id={"leaf": lax.rem(group + i, groups)},
        ).start()
    root_order((2 * blocks) // 8, (3 * blocks) // 8)
    drain(g7a, recv_sem.at[6], groups - 1)
    rrb = (-jnp.sum(g7a[...], axis=0)).astype(BF16)
    gather_start(g7b, rrb, 7)
    root_order((3 * blocks) // 8, (5 * blocks) // 8)
    loads[10].wait()
    gather_wait(g7b, 7)
    ry = dot_nt(columns(g7b), root_inv[...])
    put_product(s8, ry.astype(BF16), root_inv)
    scatter_start(s8, r8, 8)
    root_order((5 * blocks) // 8, (7 * blocks) // 8)
    root_slab = scatter_sum(r8, 8)
    gather_start(g9, root_slab.astype(BF16), 9)
    root_order((7 * blocks) // 8, blocks)
    gather_wait(g9, 9)

    pt = dot(columns(g9), panel_root[...])
    pvb = (py - pt).astype(BF16)
    put_product(s11, pvb, parent_inv)
    scatter_start(s11, r11, 11)
    rxb = get_blocks(g9)
    root_anc = [
        pick(
            dot(rxb, onehot[:, s * piece : (s + 1) * piece]),
            leaf_at[:, s * piece : (s + 1) * piece],
            blocks,
        )
        for s in range(4)
    ]
    mine = jnp.where(lane_part == part, g9[slab].astype(F32), 0.0)
    root_out[...] = functools.reduce(
        lambda x, y: x + y, [mine[:, k * width : (k + 1) * width] for k in range(per_slab)]
    )
    parent_sol = scatter_sum(r11, 11)
    gather_start(g12, parent_sol.astype(BF16), 12)
    parent_out[...] = parent_sol
    gather_wait(g12, 12)

    pxb = get_blocks(g12)
    for s in range(4):
        cols = slice(s * piece, (s + 1) * piece)
        got = (root_anc[s] + pick(dot(pxb, onehot[:, cols]), leaf_at[:, cols], 0)).astype(BF16)
        terms[pl.ds(8 * s, 8), :] = dot(got, leaf_panel[pl.ds(s * piece, piece), :])
    pack_terms(s13)
    scatter_start(s13, r13, 13)
    lvb = ly - scatter_sum(r13, 13)
    none = jnp.zeros((8, LANES), F32)
    rows_of = []
    for s in range(4):
        a, b = s // 2, s % 2
        held = jnp.where(low if b == 0 else ~low, lvb[8 * a : 8 * a + 8, :], 0.0)
        rows_of.append(jnp.concatenate([held, none] if a == 0 else [none, held], axis=1))
    terms[...] = dot(jnp.concatenate(rows_of, axis=0).astype(BF16), leaf_inv[...])
    pack_terms(s14)
    scatter_start(s14, r14, 14)
    result = scatter_sum(r14, 14)
    for a in range(2):
        rows = result[8 * a : 8 * a + 8, :]
        leaf_out[:, 2 * a, :] = rows[:, :HALF]
        leaf_out[:, 2 * a + 1, :] = swap_halves(rows)[:, :HALF]

    for phase, ref in enumerate(
        (g1, g2, r3p, g4, all_rows, r6, g7a, g7b, r8, g9, r3r, r11, g12, r13, r14, panel_cols)
    ):
        drain(ref, send_sem.at[phase], (groups if phase == 6 else n) - 1)


def store(count, *refs):
    copies = [
        pltpu.make_async_copy(refs[i], refs[count + i], refs[-1].at[i]) for i in range(count)
    ]
    for copy in copies:
        copy.start()
    for copy in copies:
        copy.wait()


def solution(mesh):
    n = mesh.shape["rows"]
    groups = mesh.shape["leaf"]

    def shards(
        leaf_rhs,
        parent_rhs,
        root_rhs,
        leaf_inv,
        leaf_panel,
        leaf_rows,
        leaf_height,
        parent_inv,
        parent_panel,
        parent_rows,
        parent_height,
        root_inv,
    ):
        leaf_cols = leaf_inv.shape[2]
        cols = root_inv.shape[1]
        height = 4 * leaf_panel.shape[1]
        packed = (16, LANES)
        vmem = pl.BlockSpec(memory_space=pltpu.VMEM)
        hbm = pl.BlockSpec(memory_space=pltpu.HBM)
        slabs = (n, 8, LANES)
        buffers = [
            ((n, *packed), BF16),
            ((n, *packed), BF16),
            (slabs, BF16),
            (slabs, BF16),
            (slabs, BF16),
            (slabs, BF16),
            (slabs, BF16),
            (slabs, BF16),
            (slabs, BF16),
            ((groups, 8, LANES), F32),
            (slabs, BF16),
            (slabs, BF16),
            (slabs, BF16),
            (slabs, BF16),
            (slabs, BF16),
            (slabs, BF16),
            (slabs, BF16),
            ((n, *packed), BF16),
            ((n, *packed), BF16),
            ((n, *packed), BF16),
            ((n, *packed), BF16),
        ]
        leaf_out, parent_out, root_out = pl.pallas_call(
            functools.partial(kernel, n, groups),
            out_shape=(
                jax.ShapeDtypeStruct((8, 4, HALF), F32),
                jax.ShapeDtypeStruct((8, LANES), F32),
                jax.ShapeDtypeStruct(root_rhs.shape, F32),
            ),
            in_specs=[hbm] * 12,
            out_specs=(vmem, vmem, vmem),
            scratch_shapes=[
                pltpu.VMEM(leaf_rhs.shape, F32),
                pltpu.VMEM((8, LANES), F32),
                pltpu.VMEM(root_rhs.shape, F32),
                pltpu.VMEM(leaf_rows.shape, jnp.int32),
                pltpu.SMEM(leaf_height.shape, jnp.int32),
                pltpu.VMEM(parent_rows.shape, jnp.int32),
                pltpu.SMEM(parent_height.shape, jnp.int32),
                pltpu.VMEM((256, leaf_cols), BF16),
                pltpu.VMEM((height, leaf_cols), BF16),
                pltpu.VMEM((LANES, cols), BF16),
                pltpu.VMEM((n, LANES, LANES), BF16),
                pltpu.VMEM((LANES, cols), BF16),
                pltpu.VMEM((n, LANES, LANES), BF16),
                pltpu.VMEM((n, 1, LANES), jnp.int32),
                pltpu.VMEM((WIDE, height), BF16),
                pltpu.VMEM((WIDE, cols), BF16),
                pltpu.VMEM((32, leaf_cols), BF16),
                pltpu.VMEM((cols, LANES), BF16),
                pltpu.VMEM((32, leaf_cols), F32),
            ]
            + [pltpu.VMEM(shape, kind) for shape, kind in buffers]
            + [
                pltpu.SemaphoreType.DMA((13,)),
                pltpu.SemaphoreType.DMA((PHASES,)),
                pltpu.SemaphoreType.DMA((PHASES,)),
            ],
            compiler_params=pltpu.CompilerParams(
                collective_id=0, has_side_effects=True, vmem_limit_bytes=48 << 20,
            ),
            name="solve",
        )(
            *(
                x if x.size == 1 else pltpu.with_memory_space_constraint(x, pltpu.HBM)
                for x in (
                    leaf_rhs,
                    parent_rhs[:, 0, :],
                    root_rhs,
                    leaf_rows,
                    leaf_height,
                    parent_rows,
                    parent_height,
                    leaf_inv.reshape(-1, leaf_cols),
                    leaf_panel.reshape(-1, leaf_cols),
                    parent_inv[0],
                    parent_panel[0],
                    root_inv,
                )
            )
        )
        results = (leaf_out, parent_out, root_out)
        leaf_out, parent_out, root_out = pl.pallas_call(
            functools.partial(store, 3),
            out_shape=tuple(jax.ShapeDtypeStruct(r.shape, r.dtype) for r in results),
            in_specs=[vmem] * 3,
            out_specs=(hbm,) * 3,
            scratch_shapes=[pltpu.SemaphoreType.DMA((3,))],
            name="store",
        )(*(pltpu.with_memory_space_constraint(r, pltpu.VMEM) for r in results))
        return leaf_out, parent_out[:, None, :], root_out

    return jax.shard_map(
        shards,
        mesh=mesh,
        in_specs=(
            P(None, "leaf", "rows"),
            P(None, "leaf", "rows"),
            P(None, ("leaf", "rows")),
            P("leaf", "rows", None),
            P("leaf", "rows", None),
            P("leaf", "rows"),
            P("leaf"),
            P("leaf", "rows", None),
            P("leaf", "rows", None),
            P("leaf", "rows"),
            P("leaf"),
            P("rows", None),
        ),
        out_specs=(P(None, "leaf", "rows"), P(None, "leaf", "rows"), P(None, ("leaf", "rows"))),
        check_vma=False,
    )
```

```python
import functools

import jax
import jax.numpy as jnp
from jax import lax
from jax.experimental import pallas as pl
from jax.experimental.pallas import tpu as pltpu
from jax.sharding import PartitionSpec as P

F32 = jnp.float32
BF16 = jnp.bfloat16
LANES = 128
HALF = 64
WIDE = 256
NT = (((1,), (1,)), ((), ()))
PHASES = 16
BULK = 15


def dot(a, b):
    return jnp.dot(a, b, preferred_element_type=F32)


def dot_nt(a, b):
    return lax.dot_general(a, b, NT, preferred_element_type=F32)


def swap_halves(x):
    return pltpu.roll(x, HALF, 1)


def kernel(
    n,
    groups,
    leaf_rhs_hbm,
    parent_rhs_hbm,
    root_rhs_hbm,
    leaf_rows_hbm,
    leaf_height_hbm,
    parent_rows_hbm,
    parent_height_hbm,
    leaf_inv_hbm,
    leaf_panel_hbm,
    parent_inv_hbm,
    parent_panel_hbm,
    root_inv_hbm,
    leaf_out,
    parent_out,
    root_out,
    leaf_rhs,
    parent_rhs,
    root_rhs,
    leaf_rows,
    leaf_height,
    parent_rows,
    parent_height,
    leaf_inv,
    leaf_panel,
    parent_inv,
    parent_panel,
    root_inv,
    panel_cols,
    all_rows,
    onehot,
    onehot_p,
    xs,
    panel_root,
    terms,
    g1,
    g2,
    s3p,
    r3p,
    s3r,
    r3r,
    g4,
    s6,
    r6,
    g7a,
    g7b,
    s8,
    r8,
    g9,
    s11,
    r11,
    g12,
    s13,
    r13,
    s14,
    r14,
    load_sem,
    send_sem,
    recv_sem,
):
    group = lax.axis_index("leaf")
    me = lax.axis_index("rows")

    barrier = pltpu.get_barrier_semaphore()

    if n == 32:
        z, x, core = lax.div(me, 8), lax.rem(lax.div(me, 2), 4), lax.rem(me, 2)
    order = [(x, c) for x in (2, 3, 1, 0) for c in (1, 0)]

    def each_peer(act):
        if n != 32:
            lax.fori_loop(1, n, lambda i, carry: (act(lax.rem(me + i, n)), carry)[1], 0)
            return

        def ring(i, carry):
            base = 8 * lax.rem(z + (2 + i) - 4 * lax.div(i, 2) + lax.div(i, 2), 4)
            for dx, dc in order:
                act(base + 2 * lax.rem(x + dx, 4) + lax.rem(core + dc, 2))
            return carry

        lax.fori_loop(0, 3, ring, 0)
        for dx, dc in order[:-1]:
            act(8 * z + 2 * lax.rem(x + dx, 4) + lax.rem(core + dc, 2))

    each_peer(lambda peer: pl.semaphore_signal(barrier, inc=1, device_id={"rows": peer}))
    for i in range(1, groups):
        pl.semaphore_signal(barrier, inc=1, device_id={"leaf": lax.rem(group + i, groups)})

    own_cols = parent_panel_hbm.at[:, pl.ds(pl.multiple_of(me * LANES, LANES), LANES)]
    loads = [
        pltpu.make_async_copy(src, dst, load_sem.at[i])
        for i, (src, dst) in enumerate(
            (
                (leaf_rhs_hbm, leaf_rhs),
                (leaf_rows_hbm, leaf_rows),
                (leaf_height_hbm, leaf_height),
                (parent_rows_hbm, parent_rows),
                (parent_height_hbm, parent_height),
                (root_rhs_hbm, root_rhs),
                (parent_rhs_hbm, parent_rhs),
                (leaf_inv_hbm, leaf_inv),
                (leaf_panel_hbm, leaf_panel),
                (parent_inv_hbm, parent_inv),
                (root_inv_hbm, root_inv),
                (own_cols, panel_cols.at[me]),
            )
        )
    ]
    for copy in loads:
        copy.start()

    def load_cols(c, carry):
        cols = pl.ds(pl.multiple_of(c * LANES, LANES), LANES)
        pltpu.make_async_copy(
            parent_panel_hbm.at[:, cols], parent_panel.at[c], load_sem.at[12]
        ).start()
        return carry

    lax.fori_loop(0, n, load_cols, 0)

    low = lax.broadcasted_iota(jnp.int32, (8, LANES), 1) < HALF
    low16 = lax.broadcasted_iota(jnp.int32, (16, LANES), 1) < HALF

    def drain(ref, sem, count):
        view = ref.at[pl.ds(0, count)]
        pltpu.make_async_copy(view, view, sem).wait()

    def gather_start(ref, value, phase):
        ref[me] = value
        each_peer(
            lambda peer: pltpu.make_async_remote_copy(
                src_ref=ref.at[me],
                dst_ref=ref.at[me],
                send_sem=send_sem.at[phase],
                recv_sem=recv_sem.at[phase],
                device_id={"rows": peer},
            ).start()
        )

    def gather_wait(ref, phase):
        drain(ref, recv_sem.at[phase], n - 1)

    def scatter_start(src, dst, phase):
        each_peer(
            lambda peer: pltpu.make_async_remote_copy(
                src_ref=src.at[peer],
                dst_ref=dst.at[me],
                send_sem=send_sem.at[phase],
                recv_sem=recv_sem.at[phase],
                device_id={"rows": peer},
            ).start()
        )
        dst[me] = src[me]

    def send_panel(turn):
        if n == 32:
            extra = {2: (2, 2), 1: (1, 3), 3: (3, 1)}[turn]
            steps = [(dz, (turn - dz) % 4) for dz in range(4)] + [extra]
            moves = [(dz, dx, dc) for dz, dx in steps for dc in range(2)]
            peers = [
                8 * lax.rem(z + dz, 4) + 2 * lax.rem(x + dx, 4) + lax.rem(core + dc, 2)
                for dz, dx, dc in moves + ([(0, 0, 1)] if turn == 2 else [])
            ]
        else:
            peers = [lax.rem(me + i, n) for i in range(turn, n, 3)]
        for peer in peers:
            pltpu.make_async_remote_copy(
                src_ref=parent_panel.at[peer],
                dst_ref=panel_cols.at[me],
                send_sem=send_sem.at[BULK],
                recv_sem=recv_sem.at[BULK],
                device_id={"rows": peer},
            ).start()

    def scatter_sum(dst, phase):
        drain(dst, recv_sem.at[phase], n - 1)
        return jnp.sum(dst[...].astype(F32), axis=0)

    def pack_rhs():
        tops = [
            jnp.concatenate([leaf_rhs[:, 2 * a, :], leaf_rhs[:, 2 * a + 1, :]], axis=1)
            for a in range(2)
        ]
        return jnp.concatenate(tops, axis=0).astype(BF16)

    def unpack(ref):
        for c in range(n // 2):
            even = ref[2 * c].astype(F32)
            odd = ref[2 * c + 1].astype(F32)
            cols = pl.ds(c * LANES, LANES)
            xs[0:16, cols] = jnp.where(low16, even, swap_halves(odd)).astype(BF16)
            xs[16:32, cols] = jnp.where(low16, swap_halves(even), odd).astype(BF16)

    def pack_terms(dst):
        for c in range(n // 2):
            cols = pl.ds(c * LANES, LANES)
            first, second = [], []
            for a in range(2):
                even = terms[pl.ds(16 * a, 8), cols]
                odd = terms[pl.ds(16 * a + 8, 8), cols]
                first.append(jnp.where(low, even, swap_halves(odd)))
                second.append(jnp.where(low, swap_halves(even), odd))
            dst[2 * c] = jnp.concatenate(first, axis=0).astype(BF16)
            dst[2 * c + 1] = jnp.concatenate(second, axis=0).astype(BF16)

    def columns(ref):
        return jnp.concatenate([ref[c] for c in range(n)], axis=1)

    blocks = n // 2

    def spread(value, where_at, first):
        pair = jnp.concatenate([value, value], axis=0).astype(BF16)
        second = lax.broadcasted_iota(jnp.int32, pair.shape, 0) >= 8
        at = jnp.concatenate([where_at, where_at], axis=0) - jnp.where(second, 1, 0)
        at = at.astype(F32).astype(BF16)
        return jnp.concatenate(
            [
                jnp.where(at == jnp.array(first + q, BF16), pair, jnp.array(0.0, BF16))
                for q in range(0, blocks, 2)
            ],
            axis=0,
        )

    def put_blocks(dst, acc):
        for c in range(n):
            part = acc[8 * (c // 2) : 8 * (c // 2) + 8, LANES * (c % 2) : LANES * (c % 2 + 1)]
            dst[c] = part.astype(dst.dtype)

    def put_product(dst, value, weights):
        for c in range(0, n, 4):
            term = dot(value, weights[:, c * LANES : (c + 4) * LANES])
            for k in range(4):
                dst[c + k] = term[:, k * LANES : (k + 1) * LANES].astype(BF16)

    def get_blocks(ref):
        return jnp.concatenate(
            [jnp.concatenate([ref[2 * q], ref[2 * q + 1]], axis=1) for q in range(blocks)], axis=0
        )

    def pick(table, where_at, first):
        total = jnp.zeros(where_at.shape, F32)
        for q in range(blocks):
            total += jnp.where(where_at == first + q, table[8 * q : 8 * q + 8, :], 0.0)
        return total

    def root_order(first, last):
        at = jnp.broadcast_to(parent_at[0:1, :], (16, n * LANES)).astype(F32).astype(BF16)
        for q in range(first, last):
            mine = at == jnp.array(q, BF16)
            chosen = jnp.concatenate(
                [
                    jnp.where(mine, onehot_p[16 * i : 16 * i + 16, :], jnp.array(0.0, BF16))
                    for i in range(WIDE // 16)
                ],
                axis=0,
            )
            panel_root[pl.ds(q * WIDE, WIDE), :] = dot(chosen, cols_of).astype(BF16)

    loads[0].wait()
    packed_rhs = pack_rhs()
    pl.semaphore_wait(barrier, n - 1 + groups - 1)
    gather_start(g1, packed_rhs, 0)
    for copy in loads[1:7]:
        copy.wait()
    pltpu.make_async_copy(parent_panel, parent_panel, load_sem.at[12]).wait()
    send_panel(2)
    all_rows[me] = parent_rows[...]
    each_peer(
        lambda peer: pltpu.make_async_remote_copy(
            src_ref=all_rows.at[me],
            dst_ref=all_rows.at[me],
            send_sem=send_sem.at[4],
            recv_sem=recv_sem.at[4],
            device_id={"rows": peer},
        ).start()
    )

    piece = leaf_rows.shape[1]
    at_list, low_list = [], []
    for s in range(4):
        rows_s = leaf_rows[s : s + 1, :]
        pos = me * piece + lax.broadcasted_iota(jnp.int32, (1, piece), 1)
        at_list.append(jnp.where(pos < leaf_height[s], rows_s >> 8, -1))
        low_list.append(rows_s & (WIDE - 1))
    height = 4 * piece
    leaf_at = jnp.broadcast_to(jnp.concatenate(at_list, axis=1), (8, height))
    leaf_low = jnp.concatenate(low_list, axis=1)
    onehot[...] = jnp.where(
        lax.broadcasted_iota(jnp.int32, (WIDE, height), 0) == leaf_low, 1.0, 0.0
    ).astype(BF16)

    loads[7].wait()
    gather_wait(g1, 0)
    unpack(g1)
    full = dot_nt(xs[...], leaf_inv[...])
    ly = jnp.concatenate(
        [
            jnp.where(low, full[0:8, 0:LANES], full[16:24, 0:LANES]),
            jnp.where(low, full[8:16, LANES:], full[24:32, LANES:]),
        ],
        axis=0,
    )
    gather_start(g2, ly.astype(BF16), 1)
    send_panel(1)

    drain(all_rows, recv_sem.at[4], n - 1)
    rows_p = jnp.concatenate([all_rows[c] for c in range(n)], axis=1)
    pos_p = lax.broadcasted_iota(jnp.int32, rows_p.shape, 1)
    parent_at = jnp.broadcast_to(
        jnp.where(pos_p < parent_height[0], rows_p >> 8, -1), (8, n * LANES)
    )
    onehot_p[...] = jnp.where(
        lax.broadcasted_iota(jnp.int32, onehot_p.shape, 0) == (rows_p & (WIDE - 1)), 1.0, 0.0
    ).astype(BF16)

    loads[8].wait()
    gather_wait(g2, 1)
    unpack(g2)
    updates = []
    acc = jnp.zeros((8 * blocks, WIDE), F32)
    for s in range(4):
        a, b = s // 2, s % 2
        cols = slice(s * piece, (s + 1) * piece)
        got = dot_nt(xs[16 * b : 16 * b + 16, :], leaf_panel[cols, :])
        updates.append(got[8 * a : 8 * a + 8, :])
        acc += dot_nt(spread(updates[s], leaf_at[:, cols], 0), onehot[:, cols])
    put_blocks(s3p, acc)
    scatter_start(s3p, r3p, 2)
    send_panel(3)
    acc = jnp.zeros((8 * blocks, WIDE), F32)
    for s in range(4):
        cols = slice(s * piece, (s + 1) * piece)
        acc += dot_nt(spread(updates[s], leaf_at[:, cols], blocks), onehot[:, cols])
    put_blocks(s3r, acc)
    pacc = scatter_sum(r3p, 2)

    prb = (parent_rhs[...] - pacc).astype(BF16)
    gather_start(g4, prb, 3)
    scatter_start(s3r, r3r, 10)
    loads[9].wait()
    loads[11].wait()
    gather_wait(g4, 3)
    py = dot_nt(columns(g4), parent_inv[...])
    drain(panel_cols, recv_sem.at[BULK], n - 1)
    cols_of = panel_cols[...].reshape(n * LANES, LANES)
    pyb = py.astype(BF16)
    acc = jnp.zeros((8 * blocks, WIDE), F32)
    chunk = 4 * LANES
    for c in range(0, n * LANES, chunk):
        cols = slice(c, c + chunk)
        got = dot_nt(pyb, cols_of[cols, :])
        acc += dot_nt(spread(got, parent_at[:, cols], 0), onehot_p[:, cols])
    put_blocks(s6, acc)
    width = root_rhs.shape[1]
    per_slab = LANES // width
    slab = lax.div(group * n + me, per_slab)
    part = lax.rem(me, per_slab)
    lane_part = lax.broadcasted_iota(jnp.int32, (8, LANES), 1) // width
    mine = jnp.concatenate([root_rhs[...]] * per_slab, axis=1)
    s6[slab] = (s6[slab].astype(F32) - jnp.where(lane_part == part, mine, 0.0)).astype(BF16)
    scatter_start(s6, r6, 5)
    root_order(0, (2 * blocks) // 8)
    racc = scatter_sum(r3r, 10)
    partial = scatter_sum(r6, 5) + racc

    g7a[group] = partial
    for i in range(1, groups):
        pltpu.make_async_remote_copy(
            src_ref=g7a.at[group],
            dst_ref=g7a.at[group],
            send_sem=send_sem.at[6],
            recv_sem=recv_sem.at[6],
            device_id={"leaf": lax.rem(group + i, groups)},
        ).start()
    root_order((2 * blocks) // 8, (3 * blocks) // 8)
    drain(g7a, recv_sem.at[6], groups - 1)
    rrb = (-jnp.sum(g7a[...], axis=0)).astype(BF16)
    gather_start(g7b, rrb, 7)
    root_order((3 * blocks) // 8, (5 * blocks) // 8)
    loads[10].wait()
    gather_wait(g7b, 7)
    ry = dot_nt(columns(g7b), root_inv[...])
    put_product(s8, ry.astype(BF16), root_inv)
    scatter_start(s8, r8, 8)
    root_order((5 * blocks) // 8, (7 * blocks) // 8)
    root_slab = scatter_sum(r8, 8)
    gather_start(g9, root_slab.astype(BF16), 9)
    root_order((7 * blocks) // 8, blocks)
    gather_wait(g9, 9)

    pt = dot(columns(g9), panel_root[...])
    pvb = (py - pt).astype(BF16)
    put_product(s11, pvb, parent_inv)
    scatter_start(s11, r11, 11)
    rxb = get_blocks(g9)
    root_anc = [
        pick(
            dot(rxb, onehot[:, s * piece : (s + 1) * piece]),
            leaf_at[:, s * piece : (s + 1) * piece],
            blocks,
        )
        for s in range(4)
    ]
    mine = jnp.where(lane_part == part, g9[slab].astype(F32), 0.0)
    root_out[...] = functools.reduce(
        lambda x, y: x + y, [mine[:, k * width : (k + 1) * width] for k in range(per_slab)]
    )
    parent_sol = scatter_sum(r11, 11)
    gather_start(g12, parent_sol.astype(BF16), 12)
    parent_out[...] = parent_sol
    gather_wait(g12, 12)

    pxb = get_blocks(g12)
    for s in range(4):
        cols = slice(s * piece, (s + 1) * piece)
        got = (root_anc[s] + pick(dot(pxb, onehot[:, cols]), leaf_at[:, cols], 0)).astype(BF16)
        terms[pl.ds(8 * s, 8), :] = dot(got, leaf_panel[pl.ds(s * piece, piece), :])
    pack_terms(s13)
    scatter_start(s13, r13, 13)
    lvb = ly - scatter_sum(r13, 13)
    none = jnp.zeros((8, LANES), F32)
    rows_of = []
    for s in range(4):
        a, b = s // 2, s % 2
        held = jnp.where(low if b == 0 else ~low, lvb[8 * a : 8 * a + 8, :], 0.0)
        rows_of.append(jnp.concatenate([held, none] if a == 0 else [none, held], axis=1))
    terms[...] = dot(jnp.concatenate(rows_of, axis=0).astype(BF16), leaf_inv[...])
    pack_terms(s14)
    scatter_start(s14, r14, 14)
    result = scatter_sum(r14, 14)
    for a in range(2):
        rows = result[8 * a : 8 * a + 8, :]
        leaf_out[:, 2 * a, :] = rows[:, :HALF]
        leaf_out[:, 2 * a + 1, :] = swap_halves(rows)[:, :HALF]

    for phase, ref in enumerate(
        (g1, g2, r3p, g4, all_rows, r6, g7a, g7b, r8, g9, r3r, r11, g12, r13, r14, panel_cols)
    ):
        drain(ref, send_sem.at[phase], (groups if phase == 6 else n) - 1)


def store(count, *refs):
    copies = [
        pltpu.make_async_copy(refs[i], refs[count + i], refs[-1].at[i]) for i in range(count)
    ]
    for copy in copies:
        copy.start()
    for copy in copies:
        copy.wait()


def solution(mesh):
    n = mesh.shape["rows"]
    groups = mesh.shape["leaf"]

    def shards(
        leaf_rhs,
        parent_rhs,
        root_rhs,
        leaf_inv,
        leaf_panel,
        leaf_rows,
        leaf_height,
        parent_inv,
        parent_panel,
        parent_rows,
        parent_height,
        root_inv,
    ):
        leaf_cols = leaf_inv.shape[2]
        cols = root_inv.shape[1]
        height = 4 * leaf_panel.shape[1]
        packed = (16, LANES)
        vmem = pl.BlockSpec(memory_space=pltpu.VMEM)
        hbm = pl.BlockSpec(memory_space=pltpu.HBM)
        slabs = (n, 8, LANES)
        buffers = [
            ((n, *packed), BF16),
            ((n, *packed), BF16),
            (slabs, BF16),
            (slabs, BF16),
            (slabs, BF16),
            (slabs, BF16),
            (slabs, BF16),
            (slabs, BF16),
            (slabs, BF16),
            ((groups, 8, LANES), F32),
            (slabs, BF16),
            (slabs, BF16),
            (slabs, BF16),
            (slabs, BF16),
            (slabs, BF16),
            (slabs, BF16),
            (slabs, BF16),
            ((n, *packed), BF16),
            ((n, *packed), BF16),
            ((n, *packed), BF16),
            ((n, *packed), BF16),
        ]
        leaf_out, parent_out, root_out = pl.pallas_call(
            functools.partial(kernel, n, groups),
            out_shape=(
                jax.ShapeDtypeStruct((8, 4, HALF), F32),
                jax.ShapeDtypeStruct((8, LANES), F32),
                jax.ShapeDtypeStruct(root_rhs.shape, F32),
            ),
            in_specs=[hbm] * 12,
            out_specs=(vmem, vmem, vmem),
            scratch_shapes=[
                pltpu.VMEM(leaf_rhs.shape, F32),
                pltpu.VMEM((8, LANES), F32),
                pltpu.VMEM(root_rhs.shape, F32),
                pltpu.VMEM(leaf_rows.shape, jnp.int32),
                pltpu.SMEM(leaf_height.shape, jnp.int32),
                pltpu.VMEM(parent_rows.shape, jnp.int32),
                pltpu.SMEM(parent_height.shape, jnp.int32),
                pltpu.VMEM((256, leaf_cols), BF16),
                pltpu.VMEM((height, leaf_cols), BF16),
                pltpu.VMEM((LANES, cols), BF16),
                pltpu.VMEM((n, LANES, LANES), BF16),
                pltpu.VMEM((LANES, cols), BF16),
                pltpu.VMEM((n, LANES, LANES), BF16),
                pltpu.VMEM((n, 1, LANES), jnp.int32),
                pltpu.VMEM((WIDE, height), BF16),
                pltpu.VMEM((WIDE, cols), BF16),
                pltpu.VMEM((32, leaf_cols), BF16),
                pltpu.VMEM((cols, LANES), BF16),
                pltpu.VMEM((32, leaf_cols), F32),
            ]
            + [pltpu.VMEM(shape, kind) for shape, kind in buffers]
            + [
                pltpu.SemaphoreType.DMA((13,)),
                pltpu.SemaphoreType.DMA((PHASES,)),
                pltpu.SemaphoreType.DMA((PHASES,)),
            ],
            compiler_params=pltpu.CompilerParams(
                collective_id=0, has_side_effects=True, vmem_limit_bytes=48 << 20,
            ),
            name="solve",
        )(
            *(
                x if x.size == 1 else pltpu.with_memory_space_constraint(x, pltpu.HBM)
                for x in (
                    leaf_rhs,
                    parent_rhs[:, 0, :],
                    root_rhs,
                    leaf_rows,
                    leaf_height,
                    parent_rows,
                    parent_height,
                    leaf_inv.reshape(-1, leaf_cols),
                    leaf_panel.reshape(-1, leaf_cols),
                    parent_inv[0],
                    parent_panel[0],
                    root_inv,
                )
            )
        )
        results = (leaf_out, parent_out, root_out)
        leaf_out, parent_out, root_out = pl.pallas_call(
            functools.partial(store, 3),
            out_shape=tuple(jax.ShapeDtypeStruct(r.shape, r.dtype) for r in results),
            in_specs=[vmem] * 3,
            out_specs=(hbm,) * 3,
            scratch_shapes=[pltpu.SemaphoreType.DMA((3,))],
            name="store",
        )(*(pltpu.with_memory_space_constraint(r, pltpu.VMEM) for r in results))
        return leaf_out, parent_out[:, None, :], root_out

    return jax.shard_map(
        shards,
        mesh=mesh,
        in_specs=(
            P(None, "leaf", "rows"),
            P(None, "leaf", "rows"),
            P(None, ("leaf", "rows")),
            P("leaf", "rows", None),
            P("leaf", "rows", None),
            P("leaf", "rows"),
            P("leaf"),
            P("leaf", "rows", None),
            P("leaf", "rows", None),
            P("leaf", "rows"),
            P("leaf"),
            P("rows", None),
        ),
        out_specs=(P(None, "leaf", "rows"), P(None, "leaf", "rows"), P(None, ("leaf", "rows"))),
        check_vma=False,
    )
```
